128 devices in a mesh: dp: 8 (over x, z_lo), space: 16 (over z_hi, y, core).
Axes of the slice: x: 4, y: 4, z: 4 (z_hi: 2, z_lo: 2; z = z_hi * 2 + z_lo), core: 2. Of those that a mesh axis runs over, the one named last changes fastest.
Arguments:
- latent: bfloat16 [8, 64, 512, 320], P('dp', 'space'), may hold values from -40 to 40
- timesteps: int32 [8], P('dp'), may hold values from 0 to 999
- norm_gain: float32 [320], replicated, may hold values from 0.1 to 1.9
- norm_bias: float32 [320], replicated, may hold values from -3 to 3
- conv_weight: bfloat16 [3, 3, 320, 320], replicated, may hold values from -0.109375 to 0.109375
- conv_bias: float32 [320], replicated, may hold values from -3 to 3
- time_weight: bfloat16 [320, 320], replicated, may hold values from -0.5 to 0.5
- cotangent: bfloat16 [8, 64, 512, 320], P('dp', 'space'), may hold values from -40 to 40
Outputs:
- block_out: bfloat16 [8, 64, 512, 320], P('dp', 'space')
- latent_grad: bfloat16 [8, 64, 512, 320], P('dp', 'space')
- weight_grad: float32 [3, 3, 320, 320], replicated
- time_grad: float32 [320, 320], replicated
The draws below stay inside these ranges and needn't reach their ends.
All inputs are finite; a program needn't handle non-finite values.
Results may differ from the reference program's by a relative error of at most 0.001.
The reference program's roundings to bfloat16 on the way (of `activated` and `embedding`) count: a program that leaves them out, or rounds other values in their place, can miss the bound.
Values may be sent and summed in bfloat16 or wider, within the bound.
A program may use at most 128 MiB of HBM per device.

```python
import math
import jax
import jax.numpy as jnp
from jax import lax

CH = 320
GROUPS = 32
COLS = 512
HEIGHT = 64
IMAGES = 8


def row_profile(top_scale):
    ramp = jnp.arange(HEIGHT, dtype=jnp.float32) / max(HEIGHT - 1, 1)
    return (jnp.exp(jnp.log(top_scale) * ramp), ramp)


def draw_latent(key, part):
    first_key = jax.random.fold_in(key, 101)
    second_key = jax.random.fold_in(key, 202)
    shape = (IMAGES, HEIGHT, COLS, CH)
    noise = jnp.clip(jax.random.normal(first_key, shape, jnp.float32), -5.0, 5.0)
    top_scale = 4.0
    scales, ramp = row_profile(top_scale)
    offset = jnp.clip(jax.random.normal(second_key, (IMAGES, 1, 1, CH), jnp.float32), -3.0, 3.0)
    values = noise * scales[None, :, None, None] + 2.0 * offset * ramp[None, :, None, None]
    return jnp.clip(values, -40.0, 40.0).astype(jnp.bfloat16)


def draw_cotangent(key, part):
    first_key = jax.random.fold_in(key, 303)
    shape = (IMAGES, HEIGHT, COLS, CH)
    noise = jnp.clip(jax.random.normal(first_key, shape, jnp.float32), -5.0, 5.0)
    top_scale = 5.0
    scales, ramp = row_profile(top_scale)
    values = noise * scales[::-1][None, :, None, None]
    return jnp.clip(values, -40.0, 40.0).astype(jnp.bfloat16)


def set_ends(drawn, stream_key, low, top_value):
    longest = drawn.shape.index(max(drawn.shape))
    spots = []
    for shift in (0, 1):
        where = [jax.random.randint(jax.random.fold_in(stream_key, axis), (), 0, length) for axis, length in enumerate(drawn.shape)]
        where[longest] = (where[longest] + shift) % drawn.shape[longest]
        spots.append(tuple(where))
    return drawn.at[spots[0]].set(low).at[spots[1]].set(top_value)


def bell_draw(own_key, shape, width, bound, kind=jnp.bfloat16):
    return jnp.clip(width * jax.random.normal(own_key, shape, jnp.float32), -bound, bound).astype(kind)


def setup_inputs(seed: int = 0) -> dict:
    seeds = jax.random.split(jax.random.key(seed), 9)
    latent = draw_latent(jax.random.fold_in(seeds[8], 71), 0)
    timesteps = set_ends(jax.random.randint(seeds[1], (IMAGES,), 0, 1000), jax.random.fold_in(seeds[1], 1), 0, 999).astype(jnp.int32)
    norm_gain = jnp.clip(1.0 + 0.18 * jax.random.normal(seeds[2], (CH,), jnp.float32), 0.1, 1.9)
    norm_bias = bell_draw(seeds[3], (CH,), 0.5, 3.0, jnp.float32)
    conv_weight = bell_draw(seeds[4], (3, 3, CH, CH), (9 * CH) ** -0.5, 0.109375)
    conv_bias = bell_draw(seeds[5], (CH,), 0.5, 3.0, jnp.float32)
    time_weight = bell_draw(seeds[6], (CH, CH), (CH // 2) ** -0.5, 0.5)
    cotangent = draw_cotangent(jax.random.fold_in(seeds[8], 71), 0)
    return {"latent": latent, "timesteps": timesteps, "norm_gain": norm_gain, "norm_bias": norm_bias, "conv_weight": conv_weight, "conv_bias": conv_bias, "time_weight": time_weight, "cotangent": cotangent}


epsilon = 1e-05

def group_stats(values):
    grouped = values.reshape(-1, GROUPS, CH // GROUPS)
    group_mean = lax.optimization_barrier(jnp.mean(grouped, axis=(0, 2)))
    centered = grouped - group_mean[None, :, None]
    group_var = lax.optimization_barrier(jnp.mean(centered * centered, axis=(0, 2)))
    return (group_mean, group_var)

def per_channel(values):
    return jnp.repeat(values, CH // GROUPS)

def sinusoid(step_value):
    half_count = CH // 2
    frequency = jnp.exp(-math.log(10000.0) * jnp.arange(half_count, dtype=jnp.float32) / half_count)
    angles = step_value.astype(jnp.float32) * frequency
    return jnp.concatenate([jnp.cos(angles), jnp.sin(angles)]).astype(jnp.bfloat16)

def one_image(latent_img, step_value, grad_img, norm_gain, norm_bias, conv_weight, conv_bias, time_weight):
    latent_wide = latent_img.astype(jnp.float32)
    group_mean, group_var = group_stats(latent_wide)
    inverse_std = lax.rsqrt(group_var + epsilon)
    normed = (latent_wide - per_channel(group_mean)) * per_channel(inverse_std)
    shifted = normed * norm_gain + norm_bias
    sigmoid_act = jax.nn.sigmoid(shifted)
    activated = (shifted * sigmoid_act).astype(jnp.bfloat16)
    padded_act = jnp.pad(activated, ((1, 1), (1, 1), (0, 0)))
    padded_grad = jnp.pad(grad_img, ((1, 1), (1, 1), (0, 0)))
    grad_flat = grad_img.reshape(-1, CH)
    conv_out = jnp.zeros((HEIGHT * COLS, CH), jnp.float32)
    act_grad = jnp.zeros((HEIGHT * COLS, CH), jnp.float32)
    weight_rows = []
    for tap_row in range(3):
        weight_cols = []
        for tap_col in range(3):
            piece = padded_act[tap_row:tap_row + HEIGHT, tap_col:tap_col + COLS].reshape(-1, CH)
            conv_out = conv_out + jnp.dot(piece, conv_weight[tap_row, tap_col], preferred_element_type=jnp.float32)
            grad_piece = padded_grad[2 - tap_row:2 - tap_row + HEIGHT, 2 - tap_col:2 - tap_col + COLS].reshape(-1, CH)
            act_grad = act_grad + jnp.dot(grad_piece, conv_weight[tap_row, tap_col].T, preferred_element_type=jnp.float32)
            weight_cols.append(jnp.dot(piece.T, grad_flat, preferred_element_type=jnp.float32))
        weight_rows.append(jnp.stack(weight_cols))
    weight_part = jnp.stack(weight_rows)
    embedding = sinusoid(step_value)
    time_bias = jnp.dot(embedding[None, :], time_weight, preferred_element_type=jnp.float32)[0]
    block_out = (latent_wide + conv_out.reshape(HEIGHT, COLS, CH) + conv_bias + time_bias).astype(jnp.bfloat16)
    act_grad = act_grad.reshape(HEIGHT, COLS, CH)
    normed_grad = act_grad * sigmoid_act * (1.0 + shifted * (1.0 - sigmoid_act)) * norm_gain
    first_mean = lax.optimization_barrier(jnp.mean(normed_grad.reshape(-1, GROUPS, CH // GROUPS), axis=(0, 2)))
    second_mean = lax.optimization_barrier(jnp.mean((normed_grad * normed).reshape(-1, GROUPS, CH // GROUPS), axis=(0, 2)))
    change = per_channel(inverse_std) * (normed_grad - per_channel(first_mean) - normed * per_channel(second_mean))
    latent_grad = (grad_img.astype(jnp.float32) + change).astype(jnp.bfloat16)
    grad_total = lax.optimization_barrier(jnp.sum(grad_img.astype(jnp.float32), axis=(0, 1)))
    time_part = embedding.astype(jnp.float32)[:, None] * grad_total[None, :]
    return (block_out, latent_grad, weight_part, time_part)

def reference(latent, timesteps, norm_gain, norm_bias, conv_weight, conv_bias, time_weight, cotangent):

    def per_image(items):
        return one_image(items[0], items[1], items[2], norm_gain, norm_bias, conv_weight, conv_bias, time_weight)
    block_out, latent_grad, weight_parts, time_parts = lax.map(per_image, (latent, timesteps, cotangent))
    return (block_out, latent_grad, lax.optimization_barrier(jnp.sum(weight_parts, axis=0)), lax.optimization_barrier(jnp.sum(time_parts, axis=0)))
```

```python
import math

import jax
import jax.numpy as jnp
from jax import lax
from jax.experimental import pallas as pl
from jax.experimental.pallas import tpu as pltpu
from jax.sharding import PartitionSpec as P

GROUPS = 32
EPSILON = 1e-05
CH = 320
ROWS = 4
COLS = 512
CELLS = ROWS * COLS
PER_GROUP = CH // GROUPS
SPACE = 16
DP = 8
TILE = 256
TILES = CELLS // TILE
MESH = pl.DeviceIdType.MESH
F32 = jnp.float32
BF16 = jnp.bfloat16

HALO = 0
STATS = 4
BACK = STATS + 15
TIME = BACK + 15
REDUCE = TIME + 7
PER_COLOUR = 17
REMOTE = REDUCE + 3 * PER_COLOUR


def device_at(x, y, z, core):
    return (x * 2 + lax.rem(z, 2), lax.div(z, 2) * 8 + y * 2 + core)


def kernel(
    emb_hbm, x_hbm, g_hbm, w_hbm, tw_hbm, gain_hbm, nbias_hbm, cbias_hbm,
    out_hbm, lg_hbm, wg_hbm, tg_hbm,
    xb, gb, wb, wt, tw, emb, gain, nbias, cbias,
    g3, a3, at, ng, mean_s, inv_s, outb, lgb, wgo, tgo,
    st_out, st_rx, bk_out, bk_rx, tm_out, tm_rx,
    wg, rx0, rx1, s1, rx2, s2, rx3, fin, res,
    bacc, local, send, recv,
):
    dp = lax.axis_index("dp")
    sp = lax.axis_index("space")
    x = lax.div(dp, 2)
    z = lax.div(sp, 8) * 2 + lax.rem(dp, 2)
    y = lax.rem(lax.div(sp, 2), 4)
    core = lax.rem(sp, 2)
    other = 1 - core
    place = {"x": x, "y": y, "z": z}

    def along(axis, d):
        spot = dict(place)
        spot[axis] = lax.rem(place[axis] + d, 4)
        return spot[axis], device_at(spot["x"], spot["y"], spot["z"], core)

    def space_peer(d):
        return (dp, lax.rem(sp + d, SPACE))

    def dp_peer(d):
        return (lax.rem(dp + d, DP), sp)

    partner = (dp, sp + 1 - 2 * core)

    def remote(number, src, dst, device):
        return pltpu.make_async_remote_copy(
            src_ref=src, dst_ref=dst, send_sem=send.at[number], recv_sem=recv.at[number],
            device_id=device, device_id_type=MESH,
        )

    def load(number, src, dst):
        return pltpu.make_async_copy(src, dst, local.at[number])

    loads = {
        "x": load(0, x_hbm, xb.at[pl.ds(COLS, CELLS)]),
        "g": load(1, g_hbm, gb.at[pl.ds(COLS, CELLS)]),
        "tw": load(2, tw_hbm, tw),
        "emb": load(3, emb_hbm, emb),
        "gain": load(4, gain_hbm, gain),
        "nbias": load(5, nbias_hbm, nbias),
        "cbias": load(6, cbias_hbm, cbias),
        "w0": load(7, w_hbm.at[0], wb.at[0, pl.ds(0, 960)]),
        "w1": load(8, w_hbm.at[1], wb.at[1, pl.ds(0, 960)]),
        "w2": load(9, w_hbm.at[2], wb.at[2, pl.ds(0, 960)]),
    }
    for name in loads:
        loads[name].start()

    barrier = pltpu.get_barrier_semaphore()
    peers = [space_peer(d) for d in range(1, SPACE)] + [dp_peer(d) for d in range(1, DP)]
    peers.append(device_at(x, y, 3 - z, core))
    for peer in peers:
        pl.semaphore_signal(barrier, inc=1, device_id=peer, device_id_type=MESH)

    for i in range(3):
        wb[i, pl.ds(960, 64), :] = jnp.zeros((64, CH), BF16)
        wt[i, pl.ds(960, 64), :] = jnp.zeros((64, CH), BF16)

    @pl.when(sp == 0)
    def _():
        gb[pl.ds(0, COLS), :] = jnp.zeros((COLS, CH), BF16)

    @pl.when(sp == SPACE - 1)
    def _():
        gb[pl.ds(5 * COLS, COLS), :] = jnp.zeros((COLS, CH), BF16)

    loads["x"].wait()
    loads["g"].wait()
    pl.semaphore_wait(barrier, len(peers))

    first, last = pl.ds(COLS, COLS), pl.ds(4 * COLS, COLS)
    above, below = pl.ds(0, COLS), pl.ds(5 * COLS, COLS)
    up = (dp, lax.max(sp - 1, 0))
    down = (dp, lax.min(sp + 1, SPACE - 1))
    g_up = remote(HALO, gb.at[first], gb.at[below], up)
    g_down = remote(HALO + 1, gb.at[last], gb.at[above], down)
    x_up = remote(HALO + 2, xb.at[first], xb.at[below], up)
    x_down = remote(HALO + 3, xb.at[last], xb.at[above], down)

    @pl.when(sp > 0)
    def _():
        g_up.start()
        x_up.start()

    @pl.when(sp < SPACE - 1)
    def _():
        g_down.start()
        x_down.start()

    step = 64

    def sums(k, carry):
        at_rows = pl.ds(pl.multiple_of(COLS + k * step, step), step)
        xs = xb[at_rows, :].astype(F32).reshape(step // 8, 8, CH)
        gs = gb[at_rows, :].astype(F32).reshape(step // 8, 8, CH)
        return carry[0] + jnp.sum(xs, axis=0), carry[1] + jnp.sum(gs, axis=0)

    zero8 = jnp.zeros((8, CH), F32)
    x_sum, g_sum = lax.fori_loop(0, CELLS // step, sums, (zero8, zero8))
    x_mean = jnp.sum(x_sum, axis=0, keepdims=True) * (1.0 / CELLS)
    g_total = jnp.sum(g_sum, axis=0, keepdims=True)

    def squares(k, carry):
        at_rows = pl.ds(pl.multiple_of(COLS + k * step, step), step)
        xs = xb[at_rows, :].astype(F32) - x_mean
        return carry + jnp.sum((xs * xs).reshape(step // 8, 8, CH), axis=0)

    x_m2 = jnp.sum(lax.fori_loop(0, CELLS // step, squares, zero8), axis=0, keepdims=True)
    st_out[0, :, pl.ds(0, CH)] = x_mean
    st_out[0, :, pl.ds(384, CH)] = x_m2
    st_out[0, :, pl.ds(768, CH)] = g_total

    def gather_space(base, out, rx):
        return [
            remote(base + d - 1, out.at[0], rx.at[sp], space_peer(d)) for d in range(1, SPACE)
        ]

    stats = gather_space(STATS, st_out, st_rx)
    for copy in stats:
        copy.start()
    st_rx[sp] = st_out[0]

    at_col = lax.broadcasted_iota(jnp.int32, (COLS, CH), 0)

    def three(row, towards):
        before = jnp.where(at_col == 0, 0.0, pltpu.roll(row, 1, 0))
        after = jnp.where(at_col == COLS - 1, 0.0, pltpu.roll(row, COLS - 1, 0))
        pieces = (before, row, after) if towards else (after, row, before)
        return jnp.concatenate(
            [*pieces, jnp.zeros((COLS, 64), F32)], axis=1
        ).astype(BF16)

    def spread_g(k, carry):
        at_rows = pl.ds(pl.multiple_of(k * COLS, COLS), COLS)
        g3[at_rows, :] = three(gb[at_rows, :].astype(F32), False)
        return carry

    lax.fori_loop(1, 5, spread_g, 0)
    for name in ("w0", "w1", "w2"):
        loads[name].wait()

    def turn(k, carry):
        i, j = lax.div(k, 3), lax.rem(k, 3)
        rows = pl.ds(pl.multiple_of(j * CH, CH), CH)
        wt[i, rows, :] = wb[i, rows, :].astype(F32).T.astype(BF16)
        return carry

    lax.fori_loop(0, 9, turn, 0)

    @pl.when(sp > 0)
    def _():
        g_up.wait_send()
        g_down.wait_recv()

    @pl.when(sp < SPACE - 1)
    def _():
        g_down.wait_send()
        g_up.wait_recv()

    spread_g(0, 0)
    spread_g(5, 0)

    row_of = lax.broadcasted_iota(jnp.int32, (CH, CH), 0)
    col_of = lax.broadcasted_iota(jnp.int32, (CH, CH), 1)
    same = (lax.shift_right_logical(row_of * 6554, 16) == lax.shift_right_logical(col_of * 6554, 16))
    member = same.astype(F32)

    def over_group(rows):
        return jnp.dot(
            jnp.broadcast_to(rows, (8, CH)), member,
            precision=lax.Precision.HIGHEST, preferred_element_type=F32,
        )[0:1]

    for name in ("gain", "nbias", "cbias", "emb", "tw"):
        loads[name].wait()
    for copy in stats:
        copy.wait()
    means = [st_rx[s, :, pl.ds(0, CH)] for s in range(SPACE)]
    total = means[0]
    for s in range(1, SPACE):
        total = total + means[s]
    mean = over_group(total) * (1.0 / (SPACE * PER_GROUP))
    spread = jnp.zeros((1, CH), F32)
    g_all = jnp.zeros((1, CH), F32)
    for s in range(SPACE):
        away = means[s] - mean
        spread = spread + (st_rx[s, :, pl.ds(384, CH)] + float(CELLS) * (away * away))
        g_all = g_all + st_rx[s, :, pl.ds(768, CH)]
    var = over_group(spread) * (1.0 / (SPACE * PER_GROUP * CELLS))
    inv = lax.rsqrt(var + EPSILON)
    mean_s[...] = mean
    inv_s[...] = inv
    gains, nbiases = gain[...], nbias[...]

    tm_out[0, :, pl.ds(0, CH)] = emb[...]
    tm_out[0, :, pl.ds(384, CH)] = g_all
    times = [
        remote(TIME + d - 1, tm_out.at[0], tm_rx.at[dp], dp_peer(d)) for d in range(1, DP)
    ]
    for copy in times:
        copy.start()
    tm_rx[dp] = tm_out[0]

    def activate(k):
        at_rows = pl.ds(pl.multiple_of(k * COLS, COLS), COLS)
        shifted = (xb[at_rows, :].astype(F32) - mean) * inv * gains + nbiases
        return shifted * jax.nn.sigmoid(shifted)

    def spread_a(k, carry):
        act = activate(k)
        a3[pl.ds(pl.multiple_of(k * COLS, COLS), COLS), :] = three(act, True)
        at[:, pl.ds(pl.multiple_of((k - 1) * COLS, COLS), COLS)] = act.T.astype(BF16)
        return carry

    lax.fori_loop(1, 5, spread_a, 0)

    orders = (("x", "y", "z"), ("y", "z", "x"), ("z", "x", "y"))
    mine = pl.ds(core * 4, 4)
    theirs = pl.ds(other * 4, 4)

    def stage(number, c):
        base = REDUCE + c * PER_COLOUR
        first_axis, second_axis, third_axis = orders[c]
        qa, qb, qc = place[first_axis], place[second_axis], place[third_axis]
        if number == 0:
            return [remote(base, wg.at[c, :, theirs], rx0.at[c], partner)]
        if number == 6:
            return [remote(base + 16, res.at[c, :, mine], res.at[c, :, mine], partner)]
        copies = []
        for d in range(1, 4):
            n = base + 1 + (number - 1) * 3 + d - 1
            if number == 1:
                to, device = along(first_axis, d)
                copies.append(remote(n, wg.at[c, to, mine], rx1.at[c, d - 1], device))
            elif number == 2:
                to, device = along(second_axis, d)
                copies.append(remote(n, s1.at[c, to], rx2.at[c, d - 1], device))
            elif number == 3:
                to, device = along(third_axis, d)
                copies.append(remote(n, s2.at[c], rx3.at[c, qc], device))
            elif number == 4:
                to, device = along(second_axis, d)
                copies.append(remote(n, fin.at[c], res.at[c, qa, core * 4 + qb], device))
            else:
                to, device = along(first_axis, d)
                piece = res.at[c, qa, mine]
                copies.append(remote(n, piece, piece, device))
        return copies

    def start(number, c):
        for copy in stage(number, c):
            copy.start()

    def event(number, c):
        first_axis, second_axis, third_axis = orders[c]
        qa, qb, qc = place[first_axis], place[second_axis], place[third_axis]
        for copy in stage(number, c):
            copy.wait()
        if number == 0:
            wg[c, :, mine] = wg[c, :, mine] + rx0[c]
        elif number == 1:
            s1[c] = wg[c, qa, mine] + rx1[c, 0] + rx1[c, 1] + rx1[c, 2]
        elif number == 2:
            total = s1[c, qb] + rx2[c, 0] + rx2[c, 1] + rx2[c, 2]
            s2[c] = total
            rx3[c, qc] = total
        elif number == 3:
            total = rx3[c, 0] + rx3[c, 1] + rx3[c, 2] + rx3[c, 3]
            fin[c] = total
            res[c, qa, core * 4 + qb] = total
        if number < 6:
            start(number + 1, c)
        else:
            q = [res[c, n].reshape(CH, 256) for n in range(4)]
            wgo[c, 0] = jnp.concatenate([q[0], q[1][:, :64]], axis=1)
            wgo[c, 1] = jnp.concatenate([q[1][:, 64:], q[2][:, :128]], axis=1)
            wgo[c, 2] = jnp.concatenate([q[2][:, 128:], q[3][:, :192]], axis=1)
            load(10 + c, wgo.at[c], wg_hbm.at[c]).start()

    def weight_part(c):
        def quarter(n, carry):
            lanes = pl.ds(pl.multiple_of(n * 256, 256), 256)
            part = jnp.dot(
                at[...], g3[pl.ds((2 - c) * COLS, CELLS), lanes], preferred_element_type=F32
            )
            wg[c, n] = part.reshape(8, 40, 256)
            return carry

        lax.fori_loop(0, 4, quarter, 0)
        start(0, c)

    for c in range(3):
        weight_part(c)

    @pl.when(sp > 0)
    def _():
        x_up.wait_send()
        x_down.wait_recv()
        a3[pl.ds(0, COLS), :] = three(activate(0), True)

    @pl.when(sp == 0)
    def _():
        a3[pl.ds(0, COLS), :] = jnp.zeros((COLS, 1024), BF16)

    @pl.when(sp < SPACE - 1)
    def _():
        x_down.wait_send()
        x_up.wait_recv()
        a3[pl.ds(5 * COLS, COLS), :] = three(activate(5), True)

    @pl.when(sp == SPACE - 1)
    def _():
        a3[pl.ds(5 * COLS, COLS), :] = jnp.zeros((COLS, 1024), BF16)

    def back_tile(t):
        at_rows = pl.ds(pl.multiple_of(t * TILE, TILE), TILE)
        grad = jnp.zeros((TILE, CH), F32)
        for i in range(3):
            rows = pl.ds(pl.multiple_of(t * TILE + (2 - i) * COLS, TILE), TILE)
            grad = grad + jnp.dot(g3[rows, :], wt[i], preferred_element_type=F32)
        xs = xb[pl.ds(pl.multiple_of(t * TILE + COLS, TILE), TILE), :].astype(F32)
        normed = (xs - mean) * inv
        shifted = normed * gains + nbiases
        sig = jax.nn.sigmoid(shifted)
        n_grad = grad * sig * (1.0 + shifted * (1.0 - sig)) * gains
        ng[at_rows, :] = n_grad
        bacc[0] += jnp.sum(n_grad.reshape(TILE // 8, 8, CH), axis=0)
        bacc[1] += jnp.sum((n_grad * normed).reshape(TILE // 8, 8, CH), axis=0)

    bacc[...] = jnp.zeros((2, 8, CH), F32)
    time_bias = jnp.dot(
        jnp.broadcast_to(emb[...], (16, CH)).astype(BF16), tw[...], preferred_element_type=F32
    )[0:1]

    def out_tile(t):
        at_rows = pl.ds(pl.multiple_of(t * TILE, TILE), TILE)
        conv = jnp.zeros((TILE, CH), F32)
        for i in range(3):
            rows = pl.ds(pl.multiple_of(t * TILE + i * COLS, TILE), TILE)
            conv = conv + jnp.dot(a3[rows, :], wb[i], preferred_element_type=F32)
        xs = xb[pl.ds(pl.multiple_of(t * TILE + COLS, TILE), TILE), :].astype(F32)
        outb[at_rows, :] = (xs + conv + cbias[...] + time_bias).astype(BF16)

    events = [(number, c) for number in range(7) for c in range(3)]

    def back_loop(t, carry):
        back_tile(t)
        for k in range(TILES):
            @pl.when(t == k)
            def _(k=k):
                event(*events[k])
        return carry

    lax.fori_loop(0, TILES, back_loop, 0)
    bk_out[0, :, pl.ds(0, CH)] = jnp.sum(bacc[0], axis=0, keepdims=True)
    bk_out[0, :, pl.ds(384, CH)] = jnp.sum(bacc[1], axis=0, keepdims=True)
    backs = gather_space(BACK, bk_out, bk_rx)
    for copy in backs:
        copy.start()
    bk_rx[sp] = bk_out[0]

    def out_loop(t, carry):
        out_tile(t)
        for k in range(TILES):
            @pl.when(t == k)
            def _(k=k):
                event(*events[TILES + k])
        return carry

    lax.fori_loop(0, TILES, out_loop, 0)
    out_copy = load(13, outb, out_hbm)
    out_copy.start()

    for copy in backs:
        copy.wait()
    first_sum, second_sum = bk_rx[0, :, pl.ds(0, CH)], bk_rx[0, :, pl.ds(384, CH)]
    for s in range(1, SPACE):
        first_sum = first_sum + bk_rx[s, :, pl.ds(0, CH)]
        second_sum = second_sum + bk_rx[s, :, pl.ds(384, CH)]
    scale = 1.0 / (SPACE * PER_GROUP * CELLS)
    first_mean = over_group(first_sum) * scale
    second_mean = over_group(second_sum) * scale

    def grad_tile(t, carry):
        at_rows = pl.ds(pl.multiple_of(t * step, step), step)
        from_rows = pl.ds(pl.multiple_of(t * step + COLS, step), step)
        normed = (xb[from_rows, :].astype(F32) - mean) * inv
        change = inv * (ng[at_rows, :] - first_mean - normed * second_mean)
        lgb[at_rows, :] = (gb[from_rows, :].astype(F32) + change).astype(BF16)
        return carry

    lax.fori_loop(0, CELLS // step, grad_tile, 0)
    lg_copy = load(14, lgb, lg_hbm)
    lg_copy.start()

    for copy in times:
        copy.wait()
    embs = jnp.concatenate([tm_rx[n, :, pl.ds(0, CH)] for n in range(DP)], axis=0)
    grads = jnp.concatenate([tm_rx[n, :, pl.ds(384, CH)] for n in range(DP)], axis=0)
    tgo[...] = lax.dot_general(
        embs, grads, (((0,), (0,)), ((), ())),
        precision=lax.Precision.HIGHEST, preferred_element_type=F32,
    )
    tg_copy = load(15, tgo, tg_hbm)
    tg_copy.start()

    for number, c in events[2 * TILES:]:
        event(number, c)
    for c in range(3):
        load(10 + c, wgo.at[c], wg_hbm.at[c]).wait()
    out_copy.wait()
    lg_copy.wait()
    tg_copy.wait()


def per_device(
    latent, timesteps, norm_gain, norm_bias, conv_weight, conv_bias, time_weight, cotangent
):
    half_count = CH // 2
    frequency = jnp.exp(-math.log(10000.0) * jnp.arange(half_count, dtype=F32) / half_count)
    angles = timesteps.astype(F32)[:, None] * frequency[None, :]
    embedding = jnp.concatenate([jnp.cos(angles), jnp.sin(angles)], axis=1).astype(BF16)
    anywhere = pl.BlockSpec(memory_space=pl.ANY)
    vmem = pltpu.VMEM
    scratch = [
        vmem((6 * COLS, CH), BF16),
        vmem((6 * COLS, CH), BF16),
        vmem((3, 1024, CH), BF16),
        vmem((3, 1024, CH), BF16),
        vmem((CH, CH), BF16),
        vmem((1, CH), F32),
        vmem((1, CH), F32),
        vmem((1, CH), F32),
        vmem((1, CH), F32),
        vmem((6 * COLS, 1024), BF16),
        vmem((6 * COLS, 1024), BF16),
        vmem((CH, CELLS), BF16),
        vmem((CELLS, CH), F32),
        vmem((1, CH), F32),
        vmem((1, CH), F32),
        vmem((CELLS, CH), BF16),
        vmem((CELLS, CH), BF16),
        vmem((3, 3, CH, CH), F32),
        vmem((CH, CH), F32),
        vmem((1, 1, 1152), F32),
        vmem((SPACE, 1, 1152), F32),
        vmem((1, 1, 768), F32),
        vmem((SPACE, 1, 768), F32),
        vmem((1, 1, 768), F32),
        vmem((DP, 1, 768), F32),
        vmem((3, 4, 8, 40, 256), F32),
        vmem((3, 4, 4, 40, 256), F32),
        vmem((3, 3, 4, 40, 256), F32),
        vmem((3, 4, 40, 256), F32),
        vmem((3, 3, 40, 256), F32),
        vmem((3, 40, 256), F32),
        vmem((3, 4, 40, 256), F32),
        vmem((3, 40, 256), F32),
        vmem((3, 4, 8, 40, 256), F32),
        vmem((2, 8, CH), F32),
        pltpu.SemaphoreType.DMA((16,)),
        pltpu.SemaphoreType.DMA((REMOTE,)),
        pltpu.SemaphoreType.DMA((REMOTE,)),
    ]
    out, lg, wgrad, tgrad = pl.pallas_call(
        kernel,
        out_shape=(
            jax.ShapeDtypeStruct((CELLS, CH), BF16),
            jax.ShapeDtypeStruct((CELLS, CH), BF16),
            jax.ShapeDtypeStruct((3, 3, CH, CH), F32),
            jax.ShapeDtypeStruct((CH, CH), F32),
        ),
        in_specs=[anywhere] * 8,
        out_specs=[anywhere] * 4,
        scratch_shapes=scratch,
        compiler_params=pltpu.CompilerParams(
            collective_id=0, has_side_effects=True, vmem_limit_bytes=60 * 1024 * 1024
        ),
        name="block",
    )(
        embedding.astype(F32),
        latent.reshape(CELLS, CH),
        cotangent.reshape(CELLS, CH),
        conv_weight.reshape(3, 3 * CH, CH),
        time_weight,
        norm_gain.reshape(1, CH),
        norm_bias.reshape(1, CH),
        conv_bias.reshape(1, CH),
    )
    shape = latent.shape
    return out.reshape(shape), lg.reshape(shape), wgrad, tgrad


def solution(mesh):
    wide = P("dp", "space", None, None)
    return jax.shard_map(
        per_device,
        mesh=mesh,
        in_specs=(wide, P("dp"), P(), P(), P(), P(), P(), wide),
        out_specs=(wide, wide, P(), P()),
        check_vma=False,
    )
```

```python
import math

import jax
import jax.numpy as jnp
from jax import lax
from jax.experimental import pallas as pl
from jax.experimental.pallas import tpu as pltpu
from jax.sharding import PartitionSpec as P

GROUPS = 32
EPSILON = 1e-05
CH = 320
ROWS = 4
COLS = 512
CELLS = ROWS * COLS
PER_GROUP = CH // GROUPS
SPACE = 16
DP = 8
DEEP = 1024
MESH = pl.DeviceIdType.MESH
F32 = jnp.float32
BF16 = jnp.bfloat16

HALO = 0
STATS = 4
BACK = STATS + 15
TIME = BACK + 15
REDUCE = TIME + 7
PER_COLOUR = 17
REMOTE = REDUCE + 3 * PER_COLOUR


def device_at(x, y, z, core):
    return (x * 2 + lax.rem(z, 2), lax.div(z, 2) * 8 + y * 2 + core)


def kernel(
    emb_hbm, x_hbm, g_hbm, w_hbm, tw_hbm, gain_hbm, nbias_hbm, cbias_hbm,
    outb, lgb, wgo, tgo,
    xb, gb, wb, tw, emb, gain, nbias, cbias,
    wgl, wcl, gt, g3, a3, at, act_s, ng, cols,
    st_out, st_rx, bk_out, bk_rx, tm_out, tm_rx,
    wg, rx0, rx1, s1, rx2, s2, rx3, fin, res,
    sums, local, send, recv,
):
    dp = lax.axis_index("dp")
    sp = lax.axis_index("space")
    x = lax.div(dp, 2)
    z = lax.div(sp, 8) * 2 + lax.rem(dp, 2)
    y = lax.rem(lax.div(sp, 2), 4)
    core = lax.rem(sp, 2)
    other = 1 - core
    place = {"x": x, "y": y, "z": z}

    def along(axis, d):
        spot = dict(place)
        spot[axis] = lax.rem(place[axis] + d, 4)
        return spot[axis], device_at(spot["x"], spot["y"], spot["z"], core)

    def space_peer(d):
        return (dp, lax.rem(sp + d, SPACE))

    def dp_peer(d):
        return (lax.rem(dp + d, DP), sp)

    partner = (dp, sp + 1 - 2 * core)

    def remote(number, src, dst, device):
        return pltpu.make_async_remote_copy(
            src_ref=src, dst_ref=dst, send_sem=send.at[number], recv_sem=recv.at[number],
            device_id=device, device_id_type=MESH,
        )

    def load(number, src, dst):
        return pltpu.make_async_copy(src, dst, local.at[number])

    loads = {
        "x": load(0, x_hbm, xb.at[pl.ds(1, ROWS)]),
        "g": load(1, g_hbm, gb.at[pl.ds(1, ROWS)]),
        "tw": load(2, tw_hbm, tw),
        "emb": load(3, emb_hbm, emb),
        "gain": load(4, gain_hbm, gain),
        "nbias": load(5, nbias_hbm, nbias),
        "cbias": load(6, cbias_hbm, cbias),
        "w": load(7, w_hbm, wb),
    }
    for name in loads:
        loads[name].start()

    barrier = pltpu.get_barrier_semaphore()
    peers = [space_peer(d) for d in range(1, SPACE)] + [dp_peer(d) for d in range(1, DP)]
    peers.append(device_at(x, y, 3 - z, core))
    for peer in peers:
        pl.semaphore_signal(barrier, inc=1, device_id=peer, device_id_type=MESH)

    for slot in range(ROWS + 2):
        rows = pl.ds(slot * DEEP + 3 * CH, DEEP - 3 * CH)
        g3[rows, :] = jnp.zeros((DEEP - 3 * CH, COLS), BF16)
        a3[rows, :] = jnp.zeros((DEEP - 3 * CH, COLS), BF16)

    @pl.when(sp == 0)
    def _():
        gb[0] = jnp.zeros((CH, COLS), BF16)

    @pl.when(sp == SPACE - 1)
    def _():
        gb[ROWS + 1] = jnp.zeros((CH, COLS), BF16)

    loads["x"].wait()
    loads["g"].wait()
    pl.semaphore_wait(barrier, len(peers))

    up = (dp, lax.max(sp - 1, 0))
    down = (dp, lax.min(sp + 1, SPACE - 1))
    g_up = remote(HALO, gb.at[1], gb.at[ROWS + 1], up)
    g_down = remote(HALO + 1, gb.at[ROWS], gb.at[0], down)
    x_up = remote(HALO + 2, xb.at[1], xb.at[ROWS + 1], up)
    x_down = remote(HALO + 3, xb.at[ROWS], xb.at[0], down)

    @pl.when(sp > 0)
    def _():
        g_up.start()
        x_up.start()

    @pl.when(sp < SPACE - 1)
    def _():
        g_down.start()
        x_down.start()

    block = 80

    def local_sums(k, carry):
        rows = pl.ds(pl.multiple_of(k * block, block), block)

        def lane_tiles(ref):
            for r in range(1, ROWS + 1):
                row = ref[r, rows, :].astype(F32)
                for n in range(COLS // 128):
                    yield row[:, n * 128 : (n + 1) * 128]

        x_sum = sum(lane_tiles(xb), jnp.zeros((block, 128), F32))
        x_mean = jnp.sum(x_sum, axis=1, keepdims=True) * (1.0 / CELLS)
        sums[0, rows, :] = jnp.broadcast_to(x_mean, (block, 128))
        squares = jnp.zeros((block, 128), F32)
        for piece in lane_tiles(xb):
            away = piece - x_mean
            squares = squares + away * away
        sums[1, rows, :] = squares
        sums[2, rows, :] = sum(lane_tiles(gb), jnp.zeros((block, 128), F32))
        return carry

    lax.fori_loop(0, CH // block, local_sums, 0)
    st_out[0, :, pl.ds(0, CH)] = sums[0].T[0:1]
    st_out[0, :, pl.ds(384, CH)] = jnp.sum(sums[1].T, axis=0, keepdims=True)
    st_out[0, :, pl.ds(768, CH)] = jnp.sum(sums[2].T, axis=0, keepdims=True)

    def gather_space(base, out, rx):
        return [
            remote(base + d - 1, out.at[0], rx.at[sp], space_peer(d)) for d in range(1, SPACE)
        ]

    stats = gather_space(STATS, st_out, st_rx)
    for copy in stats:
        copy.start()
    st_rx[sp] = st_out[0]

    at_col = lax.broadcasted_iota(jnp.int32, (CH, COLS), 1)

    def three(row, towards):
        before = jnp.where(at_col == 0, 0.0, pltpu.roll(row, 1, 1))
        after = jnp.where(at_col == COLS - 1, 0.0, pltpu.roll(row, COLS - 1, 1))
        return (before, row, after) if towards else (after, row, before)

    def spread(ref, k, pieces):
        for j in range(3):
            rows = pl.ds(pl.multiple_of(k * DEEP + j * CH, 64), CH)
            ref[rows, :] = pieces[j].astype(BF16)

    def spread_g(k, carry):
        pieces = three(gb[k].astype(F32), False)
        spread(g3, k, pieces)
        gt[pl.ds(pl.multiple_of(k * COLS, COLS), COLS), :] = jnp.concatenate(
            [*[piece.T for piece in pieces], jnp.zeros((COLS, DEEP - 3 * CH), F32)], axis=1
        ).astype(BF16)
        return carry

    lax.fori_loop(1, ROWS + 1, spread_g, 0)
    loads["w"].wait()

    def lay_out(i, carry):
        taps = wb[i].astype(F32)
        none = jnp.zeros((CH, DEEP - 3 * CH), F32)
        wcl[:, pl.ds(pl.multiple_of(i * DEEP, DEEP), DEEP)] = jnp.concatenate(
            [taps.T, none], axis=1
        ).astype(BF16)
        wgl[:, pl.ds(pl.multiple_of((2 - i) * DEEP, DEEP), DEEP)] = jnp.concatenate(
            [taps[0:CH], taps[CH : 2 * CH], taps[2 * CH :], none], axis=1
        ).astype(BF16)
        return carry

    lax.fori_loop(0, 3, lay_out, 0)

    @pl.when(sp > 0)
    def _():
        g_up.wait_send()
        g_down.wait_recv()

    @pl.when(sp < SPACE - 1)
    def _():
        g_down.wait_send()
        g_up.wait_recv()

    def ends_g(n, carry):
        return spread_g(n * (ROWS + 1), carry)

    lax.fori_loop(0, 2, ends_g, 0)

    row_of = lax.broadcasted_iota(jnp.int32, (CH, CH), 0)
    col_of = lax.broadcasted_iota(jnp.int32, (CH, CH), 1)
    same = (lax.shift_right_logical(row_of * 6554, 16) == lax.shift_right_logical(col_of * 6554, 16))
    member = same.astype(F32)

    def over_group(rows):
        return jnp.dot(
            jnp.broadcast_to(rows, (8, CH)), member,
            precision=lax.Precision.HIGHEST, preferred_element_type=F32,
        )[0:1]

    def to_column(n, rows):
        cols[n] = jnp.broadcast_to(rows, (128, CH)).T

    for name in ("gain", "nbias", "cbias", "emb", "tw"):
        loads[name].wait()
    to_column(0, gain[...].reshape(1, CH))
    to_column(1, nbias[...].reshape(1, CH))
    time_bias = jnp.dot(
        jnp.broadcast_to(emb[...].reshape(1, CH), (16, CH)).astype(BF16), tw[...],
        preferred_element_type=F32,
    )[0:1]
    to_column(2, cbias[...].reshape(1, CH) + time_bias)
    for copy in stats:
        copy.wait()
    means = [st_rx[s, :, pl.ds(0, CH)] for s in range(SPACE)]
    total = means[0]
    for s in range(1, SPACE):
        total = total + means[s]
    mean = over_group(total) * (1.0 / (SPACE * PER_GROUP))
    around = jnp.zeros((1, CH), F32)
    g_all = jnp.zeros((1, CH), F32)
    for s in range(SPACE):
        away = means[s] - mean
        around = around + (st_rx[s, :, pl.ds(384, CH)] + float(CELLS) * (away * away))
        g_all = g_all + st_rx[s, :, pl.ds(768, CH)]
    var = over_group(around) * (1.0 / (SPACE * PER_GROUP * CELLS))
    to_column(3, mean)
    to_column(4, lax.rsqrt(var + EPSILON))

    tm_out[0, :, pl.ds(0, CH)] = emb[...].reshape(1, CH)
    tm_out[0, :, pl.ds(384, CH)] = g_all
    times = [
        remote(TIME + d - 1, tm_out.at[0], tm_rx.at[dp], dp_peer(d)) for d in range(1, DP)
    ]
    for copy in times:
        copy.start()
    tm_rx[dp] = tm_out[0]

    def lanes(n):
        return pl.ds(n * 128, 128)

    def activate(k):
        for n in range(COLS // 128):
            normed = (xb[k, :, lanes(n)].astype(F32) - cols[3]) * cols[4]
            shifted = normed * cols[0] + cols[1]
            act_s[:, lanes(n)] = shifted * jax.nn.sigmoid(shifted)

    def spread_a(k, carry):
        activate(k)
        act = act_s[...]
        spread(a3, k, three(act, True))
        at[:, pl.ds(pl.multiple_of((k - 1) * COLS, COLS), COLS)] = act.astype(BF16)
        return carry

    lax.fori_loop(1, ROWS + 1, spread_a, 0)

    orders = (("x", "y", "z"), ("y", "z", "x"), ("z", "x", "y"))
    mine = pl.ds(core * 4, 4)
    theirs = pl.ds(other * 4, 4)

    def stage(number, c):
        base = REDUCE + c * PER_COLOUR
        first_axis, second_axis, third_axis = orders[c]
        qa, qb, qc = place[first_axis], place[second_axis], place[third_axis]
        if number == 0:
            return [remote(base, wg.at[c, :, theirs], rx0.at[c], partner)]
        if number == 6:
            return [remote(base + 16, res.at[c, :, mine], res.at[c, :, mine], partner)]
        copies = []
        for d in range(1, 4):
            n = base + 1 + (number - 1) * 3 + d - 1
            if number == 1:
                to, device = along(first_axis, d)
                copies.append(remote(n, wg.at[c, to, mine], rx1.at[c, d - 1], device))
            elif number == 2:
                to, device = along(second_axis, d)
                copies.append(remote(n, s1.at[c, to], rx2.at[c, d - 1], device))
            elif number == 3:
                to, device = along(third_axis, d)
                copies.append(remote(n, s2.at[c], rx3.at[c, qc], device))
            elif number == 4:
                to, device = along(second_axis, d)
                copies.append(remote(n, fin.at[c], res.at[c, qa, core * 4 + qb], device))
            else:
                to, device = along(first_axis, d)
                piece = res.at[c, qa, mine]
                copies.append(remote(n, piece, piece, device))
        return copies

    def start(number, c):
        for copy in stage(number, c):
            copy.start()

    def event(number, c):
        first_axis, second_axis, third_axis = orders[c]
        qa, qb, qc = place[first_axis], place[second_axis], place[third_axis]
        for copy in stage(number, c):
            copy.wait()
        if number == 0:
            wg[c, :, mine] = wg[c, :, mine] + rx0[c]
        elif number == 1:
            s1[c] = wg[c, qa, mine] + rx1[c, 0] + rx1[c, 1] + rx1[c, 2]
        elif number == 2:
            total = s1[c, qb] + rx2[c, 0] + rx2[c, 1] + rx2[c, 2]
            s2[c] = total
            rx3[c, qc] = total
        elif number == 3:
            total = rx3[c, 0] + rx3[c, 1] + rx3[c, 2] + rx3[c, 3]
            fin[c] = total
            res[c, qa, core * 4 + qb] = total
        if number < 6:
            start(number + 1, c)
        else:
            q = [res[c, n].reshape(CH, 256) for n in range(4)]
            wgo[c, 0] = jnp.concatenate([q[0], q[1][:, :64]], axis=1)
            wgo[c, 1] = jnp.concatenate([q[1][:, 64:], q[2][:, :128]], axis=1)
            wgo[c, 2] = jnp.concatenate([q[2][:, 128:], q[3][:, :192]], axis=1)

    def weight_part(c):
        def quarter(n, carry):
            part = jnp.dot(
                at[...],
                gt[pl.ds((2 - c) * COLS, CELLS), pl.ds(pl.multiple_of(n * 256, 256), 256)],
                preferred_element_type=F32,
            )
            wg[c, n] = part.reshape(8, 40, 256)
            return carry

        lax.fori_loop(0, 4, quarter, 0)
        start(0, c)

    for c in range(3):
        weight_part(c)

    def edge_a(k):
        activate(k)
        spread(a3, k, three(act_s[...], True))

    def blank_a(k):
        a3[pl.ds(k * DEEP, 3 * CH), :] = jnp.zeros((3 * CH, COLS), BF16)

    @pl.when(sp > 0)
    def _():
        x_up.wait_send()
        x_down.wait_recv()
        edge_a(0)

    @pl.when(sp == 0)
    def _():
        blank_a(0)

    @pl.when(sp < SPACE - 1)
    def _():
        x_down.wait_send()
        x_up.wait_recv()
        edge_a(ROWS + 1)

    @pl.when(sp == SPACE - 1)
    def _():
        blank_a(ROWS + 1)

    wide = 256
    tiles = CELLS // wide

    def spot(t):
        row = lax.div(t, 2)
        return row, pl.multiple_of(lax.rem(t, 2) * wide, wide)

    def convolve(left, right, t):
        row, col = spot(t)
        rows = pl.ds(pl.multiple_of(row * DEEP, DEEP), 3 * DEEP)
        return jnp.dot(left[...], right[rows, pl.ds(col, wide)], preferred_element_type=F32)

    def back_tile(t):
        row, col = spot(t)
        grad = convolve(wgl, g3, t)
        for n in range(wide // 128):
            here = pl.ds(col + n * 128, 128)
            normed = (xb[row + 1, :, here].astype(F32) - cols[3]) * cols[4]
            shifted = normed * cols[0] + cols[1]
            sig = jax.nn.sigmoid(shifted)
            n_grad = (
                grad[:, n * 128 : (n + 1) * 128] * sig * (1.0 + shifted * (1.0 - sig)) * cols[0]
            )
            ng[row, :, here] = n_grad
            sums[0] += n_grad
            sums[1] += n_grad * normed

    sums[0] = jnp.zeros((CH, 128), F32)
    sums[1] = jnp.zeros((CH, 128), F32)

    def out_tile(t):
        row, col = spot(t)
        conv = convolve(wcl, a3, t)
        for n in range(wide // 128):
            here = pl.ds(col + n * 128, 128)
            xs = xb[row + 1, :, here].astype(F32)
            outb[row, :, here] = (xs + conv[:, n * 128 : (n + 1) * 128] + cols[2]).astype(BF16)

    events = [(number, c) for number in range(7) for c in range(3)]

    def back_loop(t, carry):
        back_tile(t)
        for k in range(tiles):
            @pl.when(t == k)
            def _(k=k):
                event(*events[k])
        return carry

    lax.fori_loop(0, tiles, back_loop, 0)
    bk_out[0, :, pl.ds(0, CH)] = jnp.sum(sums[0].T, axis=0, keepdims=True)
    bk_out[0, :, pl.ds(384, CH)] = jnp.sum(sums[1].T, axis=0, keepdims=True)
    backs = gather_space(BACK, bk_out, bk_rx)
    for copy in backs:
        copy.start()
    bk_rx[sp] = bk_out[0]

    def out_loop(t, carry):
        out_tile(t)
        for k in range(tiles):
            @pl.when(t == k)
            def _(k=k):
                event(*events[tiles + k])
        return carry

    lax.fori_loop(0, tiles, out_loop, 0)

    for copy in backs:
        copy.wait()
    first_sum, second_sum = bk_rx[0, :, pl.ds(0, CH)], bk_rx[0, :, pl.ds(384, CH)]
    for s in range(1, SPACE):
        first_sum = first_sum + bk_rx[s, :, pl.ds(0, CH)]
        second_sum = second_sum + bk_rx[s, :, pl.ds(384, CH)]
    scale = 1.0 / (SPACE * PER_GROUP * CELLS)
    to_column(5, over_group(first_sum) * scale)
    to_column(6, over_group(second_sum) * scale)

    def grad_row(row, carry):
        for n in range(COLS // 128):
            normed = (xb[row + 1, :, lanes(n)].astype(F32) - cols[3]) * cols[4]
            change = cols[4] * (ng[row, :, lanes(n)] - cols[5] - normed * cols[6])
            lgb[row, :, lanes(n)] = (gb[row + 1, :, lanes(n)].astype(F32) + change).astype(BF16)
        return carry

    lax.fori_loop(0, ROWS, grad_row, 0)

    for copy in times:
        copy.wait()
    embs = jnp.concatenate([tm_rx[n, :, pl.ds(0, CH)] for n in range(DP)], axis=0)
    grads = jnp.concatenate([tm_rx[n, :, pl.ds(384, CH)] for n in range(DP)], axis=0)
    tgo[...] = lax.dot_general(
        embs, grads, (((0,), (0,)), ((), ())),
        precision=lax.Precision.HIGHEST, preferred_element_type=F32,
    )

    for number, c in events[2 * tiles:]:
        event(number, c)


def store(out_v, lg_v, wg_v, tg_v, out_hbm, lg_hbm, wg_hbm, tg_hbm, sems):
    pairs = ((wg_v, wg_hbm), (out_v, out_hbm), (lg_v, lg_hbm), (tg_v, tg_hbm))
    copies = [pltpu.make_async_copy(a, b, sems.at[n]) for n, (a, b) in enumerate(pairs)]
    for copy in copies:
        copy.start()
    for copy in copies:
        copy.wait()


def per_device(
    latent, timesteps, norm_gain, norm_bias, conv_weight, conv_bias, time_weight, cotangent
):
    half_count = CH // 2
    frequency = jnp.exp(-math.log(10000.0) * jnp.arange(half_count, dtype=F32) / half_count)
    angles = timesteps.astype(F32)[:, None] * frequency[None, :]
    embedding = jnp.concatenate([jnp.cos(angles), jnp.sin(angles)], axis=1).astype(BF16)
    anywhere = pl.BlockSpec(memory_space=pl.ANY)
    vmem = pltpu.VMEM
    scratch = [
        vmem((ROWS + 2, CH, COLS), BF16),
        vmem((ROWS + 2, CH, COLS), BF16),
        vmem((3, 3 * CH, CH), BF16),
        vmem((CH, CH), BF16),
        vmem((CH,), F32),
        vmem((CH,), F32),
        vmem((CH,), F32),
        vmem((CH,), F32),
        vmem((CH, 3 * DEEP), BF16),
        vmem((CH, 3 * DEEP), BF16),
        vmem(((ROWS + 2) * COLS, DEEP), BF16),
        vmem(((ROWS + 2) * DEEP, COLS), BF16),
        vmem(((ROWS + 2) * DEEP, COLS), BF16),
        vmem((CH, CELLS), BF16),
        vmem((CH, COLS), F32),
        vmem((ROWS, CH, COLS), F32),
        vmem((7, CH, 128), F32),
        vmem((1, 1, 1152), F32),
        vmem((SPACE, 1, 1152), F32),
        vmem((1, 1, 768), F32),
        vmem((SPACE, 1, 768), F32),
        vmem((1, 1, 768), F32),
        vmem((DP, 1, 768), F32),
        vmem((3, 4, 8, 40, 256), F32),
        vmem((3, 4, 4, 40, 256), F32),
        vmem((3, 3, 4, 40, 256), F32),
        vmem((3, 4, 40, 256), F32),
        vmem((3, 3, 40, 256), F32),
        vmem((3, 40, 256), F32),
        vmem((3, 4, 40, 256), F32),
        vmem((3, 40, 256), F32),
        vmem((3, 4, 8, 40, 256), F32),
        vmem((3, CH, 128), F32),
        pltpu.SemaphoreType.DMA((16,)),
        pltpu.SemaphoreType.DMA((REMOTE,)),
        pltpu.SemaphoreType.DMA((REMOTE,)),
    ]
    shapes = (
        ((ROWS, CH, COLS), BF16),
        ((ROWS, CH, COLS), BF16),
        ((3, 3, CH, CH), F32),
        ((CH, CH), F32),
    )
    held = pl.pallas_call(
        kernel,
        out_shape=tuple(vmem(*shape) for shape in shapes),
        in_specs=[anywhere] * 8,
        out_specs=[pl.BlockSpec(memory_space=pltpu.VMEM)] * 4,
        scratch_shapes=scratch,
        compiler_params=pltpu.CompilerParams(
            collective_id=0, has_side_effects=True, vmem_limit_bytes=52 * 1024 * 1024
        ),
        name="block",
    )(
        embedding.astype(F32).reshape(CH),
        jnp.swapaxes(latent, 2, 3).reshape(ROWS, CH, COLS),
        jnp.swapaxes(cotangent, 2, 3).reshape(ROWS, CH, COLS),
        conv_weight.reshape(3, 3 * CH, CH),
        time_weight,
        norm_gain,
        norm_bias,
        conv_bias,
    )
    out, lg, wgrad, tgrad = pl.pallas_call(
        store,
        out_shape=tuple(jax.ShapeDtypeStruct(*shape) for shape in shapes),
        in_specs=[anywhere] * 4,
        out_specs=[anywhere] * 4,
        scratch_shapes=[pltpu.SemaphoreType.DMA((4,))],
        compiler_params=pltpu.CompilerParams(vmem_limit_bytes=1024 * 1024),
        name="store",
    )(*held)
    out = jnp.swapaxes(out.reshape(1, ROWS, CH, COLS), 2, 3)
    lg = jnp.swapaxes(lg.reshape(1, ROWS, CH, COLS), 2, 3)
    return out, lg, wgrad, tgrad


def solution(mesh):
    wide = P("dp", "space", None, None)
    return jax.shard_map(
        per_device,
        mesh=mesh,
        in_specs=(wide, P("dp"), P(), P(), P(), P(), P(), wide),
        out_specs=(wide, wide, P(), P()),
        check_vma=False,
    )
```

```python
import math

import jax
import jax.numpy as jnp
from jax import lax
from jax.experimental import pallas as pl
from jax.experimental.pallas import tpu as pltpu
from jax.sharding import PartitionSpec as P

GROUPS = 32
EPSILON = 1e-05
CH = 320
ROWS = 4
COLS = 512
CELLS = ROWS * COLS
PER_GROUP = CH // GROUPS
SPACE = 16
DP = 8
DEEP = 1024
MESH = pl.DeviceIdType.MESH
F32 = jnp.float32
BF16 = jnp.bfloat16

HALO = 0
STATS = 4
BACK = STATS + 15
COLUMN = BACK + 15
TIME = COLUMN + 15
REDUCE = TIME + 7
PER_FLOW = 17
REMOTE = REDUCE + 6 * PER_FLOW

HALF_US, TILE_US, EVENT_US = 0.7, 0.5, 0.1
ARRIVES_US = (1.5, 4.5, 7.0, 9.5, 12.0, 15.0, 17.5)


def device_at(x, y, z, core):
    return (x * 2 + lax.rem(z, 2), lax.div(z, 2) * 8 + y * 2 + core)


def kernel(
    emb_hbm, x_hbm, g_hbm, w_hbm, tw_hbm, gain_hbm, nbias_hbm, cbias_hbm,
    outb, lgb, wgo, tgo,
    xb, gb, wb, tw, emb, gain, nbias, cbias,
    wgl, wcl, gt, g3, a3, at, act_s, ng, cols,
    st_out, st_rx, co_out, co_rx, bk_out, bk_rx, tm_out, tm_rx,
    wg, rx0, tx1, rx1, s1, rx2, s2, rx3, fin, res,
    sums, local, send, recv,
):
    dp = lax.axis_index("dp")
    sp = lax.axis_index("space")
    x = lax.div(dp, 2)
    z = lax.div(sp, 8) * 2 + lax.rem(dp, 2)
    y = lax.rem(lax.div(sp, 2), 4)
    core = lax.rem(sp, 2)
    other = 1 - core
    place = {"x": x, "y": y, "z": z}

    def along(axis, d):
        spot = dict(place)
        spot[axis] = lax.rem(place[axis] + d, 4)
        return spot[axis], device_at(spot["x"], spot["y"], spot["z"], core)

    def space_peer(d):
        return (dp, lax.rem(sp + d, SPACE))

    def dp_peer(d):
        return (lax.rem(dp + d, DP), sp)

    partner = (dp, sp + 1 - 2 * core)

    def remote(number, src, dst, device):
        return pltpu.make_async_remote_copy(
            src_ref=src, dst_ref=dst, send_sem=send.at[number], recv_sem=recv.at[number],
            device_id=device, device_id_type=MESH,
        )

    def load(number, src, dst):
        return pltpu.make_async_copy(src, dst, local.at[number])

    loads = {
        "x": load(0, x_hbm, xb.at[pl.ds(1, ROWS)]),
        "g": load(1, g_hbm, gb.at[pl.ds(1, ROWS)]),
        "tw": load(2, tw_hbm, tw),
        "emb": load(3, emb_hbm, emb),
        "gain": load(4, gain_hbm, gain),
        "nbias": load(5, nbias_hbm, nbias),
        "cbias": load(6, cbias_hbm, cbias),
        "w": load(7, w_hbm, wb),
    }
    barrier = pltpu.get_barrier_semaphore()
    peers = [space_peer(d) for d in range(1, SPACE)] + [dp_peer(d) for d in range(1, DP)]
    peers.append(device_at(x, y, 3 - z, core))
    for peer in peers:
        pl.semaphore_signal(barrier, inc=1, device_id=peer, device_id_type=MESH)

    for name in loads:
        loads[name].start()

    for slot in range(ROWS + 2):
        rows = pl.ds(slot * DEEP + 3 * CH, DEEP - 3 * CH)
        g3[rows, :] = jnp.zeros((DEEP - 3 * CH, COLS), BF16)
        a3[rows, :] = jnp.zeros((DEEP - 3 * CH, COLS), BF16)

    @pl.when(sp == 0)
    def _():
        gb[0] = jnp.zeros((CH, COLS), BF16)

    @pl.when(sp == SPACE - 1)
    def _():
        gb[ROWS + 1] = jnp.zeros((CH, COLS), BF16)

    loads["x"].wait()

    block = 80

    def lane_tiles(ref, rows):
        for r in range(1, ROWS + 1):
            row = ref[r, rows, :].astype(F32)
            for n in range(COLS // 128):
                yield row[:, n * 128 : (n + 1) * 128]

    def local_sums(k, carry):
        rows = pl.ds(pl.multiple_of(k * block, block), block)
        x_sum = sum(lane_tiles(xb, rows), jnp.zeros((block, 128), F32))
        x_mean = jnp.sum(x_sum, axis=1, keepdims=True) * (1.0 / CELLS)
        sums[0, rows, :] = jnp.broadcast_to(x_mean, (block, 128))
        squares = jnp.zeros((block, 128), F32)
        for piece in lane_tiles(xb, rows):
            away = piece - x_mean
            squares = squares + away * away
        sums[1, rows, :] = squares
        return carry

    def local_totals(k, carry):
        rows = pl.ds(pl.multiple_of(k * block, block), block)
        sums[2, rows, :] = sum(lane_tiles(gb, rows), jnp.zeros((block, 128), F32))
        return carry

    lax.fori_loop(0, CH // block, local_sums, 0)
    st_out[0, :, pl.ds(0, CH)] = sums[0].T[0:1]
    st_out[0, :, pl.ds(384, CH)] = jnp.sum(sums[1].T, axis=0, keepdims=True)

    def gather_space(base, out, rx):
        return [
            remote(base + d - 1, out.at[0], rx.at[sp], space_peer(d)) for d in range(1, SPACE)
        ]

    stats = gather_space(STATS, st_out, st_rx)
    pl.semaphore_wait(barrier, len(peers))
    for copy in stats:
        copy.start()
    st_rx[sp] = st_out[0]
    loads["g"].wait()

    up = (dp, lax.max(sp - 1, 0))
    down = (dp, lax.min(sp + 1, SPACE - 1))
    g_up = remote(HALO, gb.at[1], gb.at[ROWS + 1], up)
    g_down = remote(HALO + 1, gb.at[ROWS], gb.at[0], down)
    x_up = remote(HALO + 2, xb.at[1], xb.at[ROWS + 1], up)
    x_down = remote(HALO + 3, xb.at[ROWS], xb.at[0], down)

    @pl.when(sp > 0)
    def _():
        g_up.start()

    @pl.when(sp < SPACE - 1)
    def _():
        g_down.start()

    @pl.when(sp > 0)
    def _():
        x_up.start()

    @pl.when(sp < SPACE - 1)
    def _():
        x_down.start()

    lax.fori_loop(0, CH // block, local_totals, 0)
    co_out[0, :, :] = jnp.sum(sums[2].T, axis=0, keepdims=True)
    columns = gather_space(COLUMN, co_out, co_rx)
    for copy in columns:
        copy.start()
    co_rx[sp] = co_out[0]


    at_col = lax.broadcasted_iota(jnp.int32, (CH, COLS), 1)

    def three(row, towards):
        before = jnp.where(at_col == 0, 0.0, pltpu.roll(row, 1, 1))
        after = jnp.where(at_col == COLS - 1, 0.0, pltpu.roll(row, COLS - 1, 1))
        return (before, row, after) if towards else (after, row, before)

    def spread(ref, k, pieces):
        for j in range(3):
            rows = pl.ds(pl.multiple_of(k * DEEP + j * CH, 64), CH)
            ref[rows, :] = pieces[j].astype(BF16)

    def spread_g(k, carry):
        pieces = three(gb[k].astype(F32), False)
        spread(g3, k, pieces)
        gt[pl.ds(pl.multiple_of(k * COLS, COLS), COLS), :] = (
            g3[pl.ds(pl.multiple_of(k * DEEP, DEEP), DEEP), :].T
        )
        return carry

    lax.fori_loop(1, ROWS + 1, spread_g, 0)
    loads["w"].wait()

    def lay_out(i, carry):
        taps = wb[i].astype(F32)
        none = jnp.zeros((CH, DEEP - 3 * CH), F32)
        wcl[:, pl.ds(pl.multiple_of(i * DEEP, DEEP), DEEP)] = jnp.concatenate(
            [taps.T, none], axis=1
        ).astype(BF16)
        wgl[:, pl.ds(pl.multiple_of((2 - i) * DEEP, DEEP), DEEP)] = jnp.concatenate(
            [taps[0:CH], taps[CH : 2 * CH], taps[2 * CH :], none], axis=1
        ).astype(BF16)
        return carry

    lax.fori_loop(0, 3, lay_out, 0)

    @pl.when(sp > 0)
    def _():
        g_up.wait_send()
        g_down.wait_recv()

    @pl.when(sp < SPACE - 1)
    def _():
        g_down.wait_send()
        g_up.wait_recv()

    def ends_g(n, carry):
        return spread_g(n * (ROWS + 1), carry)

    lax.fori_loop(0, 2, ends_g, 0)

    row_of = lax.broadcasted_iota(jnp.int32, (CH, CH), 0)
    col_of = lax.broadcasted_iota(jnp.int32, (CH, CH), 1)
    same = (lax.shift_right_logical(row_of * 6554, 16) == lax.shift_right_logical(col_of * 6554, 16))
    member = same.astype(F32)

    def over_group(rows):
        return jnp.dot(
            jnp.broadcast_to(rows, (8, CH)), member,
            precision=lax.Precision.HIGHEST, preferred_element_type=F32,
        )[0:1]

    def to_column(n, rows):
        cols[n] = jnp.broadcast_to(rows, (128, CH)).T

    for name in ("gain", "nbias", "cbias", "emb", "tw"):
        loads[name].wait()
    to_column(0, gain[...].reshape(1, CH))
    to_column(1, nbias[...].reshape(1, CH))
    time_bias = jnp.dot(
        jnp.broadcast_to(emb[...].reshape(1, CH), (16, CH)).astype(BF16), tw[...],
        preferred_element_type=F32,
    )[0:1]
    to_column(2, cbias[...].reshape(1, CH) + time_bias)
    for copy in stats:
        copy.wait()
    means = [st_rx[s, :, pl.ds(0, CH)] for s in range(SPACE)]
    total = means[0]
    for s in range(1, SPACE):
        total = total + means[s]
    mean = over_group(total) * (1.0 / (SPACE * PER_GROUP))
    around = jnp.zeros((1, CH), F32)
    for s in range(SPACE):
        away = means[s] - mean
        around = around + (st_rx[s, :, pl.ds(384, CH)] + float(CELLS) * (away * away))
    var = over_group(around) * (1.0 / (SPACE * PER_GROUP * CELLS))
    to_column(3, mean)
    to_column(4, lax.rsqrt(var + EPSILON))

    def lanes(n):
        return pl.ds(n * 128, 128)

    def activate(k):
        for n in range(COLS // 128):
            normed = (xb[k, :, lanes(n)].astype(F32) - cols[3]) * cols[4]
            shifted = normed * cols[0] + cols[1]
            act_s[:, lanes(n)] = shifted * jax.nn.sigmoid(shifted)

    def spread_a(k, carry):
        activate(k)
        act = act_s[...]
        spread(a3, k, three(act, True))
        at[:, pl.ds(pl.multiple_of((k - 1) * COLS, COLS), COLS)] = act.astype(BF16)
        return carry

    lax.fori_loop(1, ROWS + 1, spread_a, 0)

    for copy in columns:
        copy.wait()
    g_all = co_rx[0]
    for n in range(1, SPACE):
        g_all = g_all + co_rx[n]
    tm_out[0, :, pl.ds(0, CH)] = emb[...].reshape(1, CH)
    tm_out[0, :, pl.ds(384, CH)] = g_all
    times = [
        remote(TIME + d - 1, tm_out.at[0], tm_rx.at[dp], dp_peer(d)) for d in range(1, DP)
    ]
    for copy in times:
        copy.start()
    tm_rx[dp] = tm_out[0]

    def to_blocks(values):
        top = jnp.max(jnp.abs(values), axis=1, keepdims=True)
        power = jnp.ceil(jnp.log2(jnp.maximum(top, 1e-30)) + 0.01)
        whole = jnp.floor(values * jnp.exp2(15.0 - power) + 0.5)
        powers = jnp.broadcast_to(power, (values.shape[0], 8, 128))
        return jnp.concatenate([whole, powers], axis=1).astype(jnp.int32).astype(jnp.int16)

    def from_blocks(blocks):
        wide_blocks = blocks.astype(jnp.int32).astype(F32)
        return wide_blocks[:, :40] * jnp.exp2(wide_blocks[:, 40:41] - 15.0)

    orders = (("x", "y", "z"), ("y", "z", "x"), ("z", "x", "y"))
    mine = pl.ds(core * 4, 4)
    theirs = pl.ds(other * 4, 4)

    def axes(f):
        names = orders[f % 3]
        return (*names, *[place[name] for name in names])

    def stage(number, f):
        base = REDUCE + f * PER_FLOW
        first_axis, second_axis, third_axis, qa, qb, qc = axes(f)
        if number == 0:
            return [remote(base, wg.at[f, :, theirs], rx0.at[f], partner)]
        if number == 6:
            return [remote(base + 16, res.at[f, :, mine], res.at[f, :, mine], partner)]
        copies = []
        for d in range(1, 4):
            n = base + 1 + (number - 1) * 3 + d - 1
            if number == 1:
                to, device = along(first_axis, d)
                copies.append(remote(n, tx1.at[f, d - 1], rx1.at[f, d - 1], device))
            elif number == 2:
                to, device = along(second_axis, d)
                copies.append(remote(n, s1.at[f, to], rx2.at[f, d - 1], device))
            elif number == 3:
                to, device = along(third_axis, d)
                copies.append(remote(n, s2.at[f], rx3.at[f, qc], device))
            elif number == 4:
                to, device = along(second_axis, d)
                copies.append(remote(n, fin.at[f], res.at[f, qa, core * 4 + qb], device))
            else:
                to, device = along(first_axis, d)
                piece = res.at[f, qa, mine]
                copies.append(remote(n, piece, piece, device))
        return copies

    def start(number, f):
        for copy in stage(number, f):
            copy.start()

    def event(number, f):
        first_axis, second_axis, third_axis, qa, qb, qc = axes(f)
        for copy in stage(number, f):
            copy.wait_recv()
        if number == 0:
            s1[f] = wg[f, qa, mine] + rx0[f, qa]
            for d in range(1, 4):
                to, _ = along(first_axis, d)
                tx1[f, d - 1] = to_blocks(wg[f, to, mine] + rx0[f, to])
        elif number == 1:
            for d in range(3):
                s1[f] += from_blocks(rx1[f, d])
        elif number == 2:
            total = s1[f, qb] + rx2[f, 0] + rx2[f, 1] + rx2[f, 2]
            s2[f] = total
            rx3[f, qc] = total
        elif number == 3:
            total = rx3[f, 0] + rx3[f, 1] + rx3[f, 2] + rx3[f, 3]
            block = to_blocks(total[None])[0]
            fin[f] = block
            res[f, qa, core * 4 + qb] = block
        if number < 6:
            start(number + 1, f)
        elif f % 2 == 1:
            c = f // 2
            part = [from_blocks(res[f - 1 + n // 4, n % 4]).reshape(CH, 128) for n in range(8)]
            wgo[c, 0] = jnp.concatenate([part[0], part[1], part[2][:, :64]], axis=1)
            wgo[c, 1] = jnp.concatenate([part[2][:, 64:], part[3], part[4]], axis=1)
            wgo[c, 2] = jnp.concatenate([part[5], part[6], part[7][:, :64]], axis=1)

    flows = 6
    due = sorted(
        (HALF_US * (f + 1) + ARRIVES_US[number], number, f)
        for number in range(7)
        for f in range(flows)
    )
    clock = [0.0]

    def work(us, do):
        while due and due[0][0] <= clock[0]:
            event(*due.pop(0)[1:])
            clock[0] += EVENT_US
        do()
        clock[0] += us

    def weight_part(f):
        c = f // 2
        for n in range((f % 2) * 2, (f % 2) * 2 + 2):
            part = jnp.dot(
                at[...],
                gt[pl.ds((2 - c) * COLS, CELLS), pl.ds(n * 256, 256)],
                preferred_element_type=F32,
            )
            for side in range(2):
                wg[f, (n % 2) * 2 + side] = part[:, side * 128 : (side + 1) * 128].reshape(
                    8, 40, 128
                )
        start(0, f)

    for f in range(flows):
        work(HALF_US, lambda f=f: weight_part(f))

    def edge_a(k):
        activate(k)
        spread(a3, k, three(act_s[...], True))

    def blank_a(k):
        a3[pl.ds(k * DEEP, 3 * CH), :] = jnp.zeros((3 * CH, COLS), BF16)

    def top_a():
        @pl.when(sp > 0)
        def _():
            x_up.wait_send()
            x_down.wait_recv()
            edge_a(0)

        @pl.when(sp == 0)
        def _():
            blank_a(0)

    def bottom_a():
        @pl.when(sp < SPACE - 1)
        def _():
            x_down.wait_send()
            x_up.wait_recv()
            edge_a(ROWS + 1)

        @pl.when(sp == SPACE - 1)
        def _():
            blank_a(ROWS + 1)

    wide = 256
    tiles = CELLS // wide

    def spot(t):
        return t // 2, (t % 2) * wide

    def convolve(left, right, t):
        row, col = spot(t)
        rows = pl.ds(row * DEEP, 3 * DEEP)
        return jnp.dot(left[...], right[rows, pl.ds(col, wide)], preferred_element_type=F32)

    def back_tile(t):
        row, col = spot(t)
        grad = convolve(wgl, g3, t)
        for n in range(wide // 128):
            here = pl.ds(col + n * 128, 128)
            normed = (xb[row + 1, :, here].astype(F32) - cols[3]) * cols[4]
            shifted = normed * cols[0] + cols[1]
            sig = jax.nn.sigmoid(shifted)
            n_grad = (
                grad[:, n * 128 : (n + 1) * 128] * sig * (1.0 + shifted * (1.0 - sig)) * cols[0]
            )
            ng[row, :, here] = n_grad
            sums[0] += n_grad
            sums[1] += n_grad * normed

    sums[0] = jnp.zeros((CH, 128), F32)
    sums[1] = jnp.zeros((CH, 128), F32)

    def out_tile(t):
        row, col = spot(t)
        conv = convolve(wcl, a3, t)
        for n in range(wide // 128):
            here = pl.ds(col + n * 128, 128)
            xs = xb[row + 1, :, here].astype(F32)
            outb[row, :, here] = (xs + conv[:, n * 128 : (n + 1) * 128] + cols[2]).astype(BF16)

    def send_back():
        bk_out[0, :, pl.ds(0, CH)] = jnp.sum(sums[0].T, axis=0, keepdims=True)
        bk_out[0, :, pl.ds(384, CH)] = jnp.sum(sums[1].T, axis=0, keepdims=True)
        for copy in gather_space(BACK, bk_out, bk_rx):
            copy.start()
        bk_rx[sp] = bk_out[0]

    def take_back():
        for copy in gather_space(BACK, bk_out, bk_rx):
            copy.wait()
        scale = 1.0 / (SPACE * PER_GROUP * CELLS)
        for n in range(2):
            total = bk_rx[0, :, pl.ds(n * 384, CH)]
            for s in range(1, SPACE):
                total = total + bk_rx[s, :, pl.ds(n * 384, CH)]
            to_column(5 + n, over_group(total) * scale)

    def grad_row(row):
        for n in range(COLS // 128):
            normed = (xb[row + 1, :, lanes(n)].astype(F32) - cols[3]) * cols[4]
            change = cols[4] * (ng[row, :, lanes(n)] - cols[5] - normed * cols[6])
            lgb[row, :, lanes(n)] = (gb[row + 1, :, lanes(n)].astype(F32) + change).astype(BF16)

    def time_gradient():
        for copy in times:
            copy.wait()
        embs = jnp.concatenate([tm_rx[n, :, pl.ds(0, CH)] for n in range(DP)], axis=0)
        grads = jnp.concatenate([tm_rx[n, :, pl.ds(384, CH)] for n in range(DP)], axis=0)
        tgo[...] = lax.dot_general(
            embs, grads, (((0,), (0,)), ((), ())),
            precision=lax.Precision.HIGHEST, preferred_element_type=F32,
        )

    for t in range(tiles):
        work(TILE_US, lambda t=t: back_tile(t))
    work(1.0, send_back)
    work(0.5, top_a)
    work(0.5, bottom_a)
    for t in range(tiles):
        work(TILE_US, lambda t=t: out_tile(t))
    work(1.0, take_back)
    for row in range(ROWS):
        work(0.4, lambda row=row: grad_row(row))
    work(1.0, time_gradient)
    while due:
        event(*due.pop(0)[1:])
    for f in range(flows):
        for number in range(7):
            for copy in stage(number, f):
                copy.wait_send()


def store(out_v, lg_v, wg_v, tg_v, out_hbm, lg_hbm, wg_hbm, tg_hbm, sems):
    pairs = ((wg_v, wg_hbm), (out_v, out_hbm), (lg_v, lg_hbm), (tg_v, tg_hbm))
    copies = [pltpu.make_async_copy(a, b, sems.at[n]) for n, (a, b) in enumerate(pairs)]
    for copy in copies:
        copy.start()
    for copy in copies:
        copy.wait()


def per_device(
    latent, timesteps, norm_gain, norm_bias, conv_weight, conv_bias, time_weight, cotangent
):
    half_count = CH // 2
    frequency = jnp.exp(-math.log(10000.0) * jnp.arange(half_count, dtype=F32) / half_count)
    angles = timesteps.astype(F32)[:, None] * frequency[None, :]
    embedding = jnp.concatenate([jnp.cos(angles), jnp.sin(angles)], axis=1).astype(BF16)
    anywhere = pl.BlockSpec(memory_space=pl.ANY)
    vmem = pltpu.VMEM
    scratch = [
        vmem((ROWS + 2, CH, COLS), BF16),
        vmem((ROWS + 2, CH, COLS), BF16),
        vmem((3, 3 * CH, CH), BF16),
        vmem((CH, CH), BF16),
        vmem((CH,), F32),
        vmem((CH,), F32),
        vmem((CH,), F32),
        vmem((CH,), F32),
        vmem((CH, 3 * DEEP), BF16),
        vmem((CH, 3 * DEEP), BF16),
        vmem(((ROWS + 2) * COLS, DEEP), BF16),
        vmem(((ROWS + 2) * DEEP, COLS), BF16),
        vmem(((ROWS + 2) * DEEP, COLS), BF16),
        vmem((CH, CELLS), BF16),
        vmem((CH, COLS), F32),
        vmem((ROWS, CH, COLS), F32),
        vmem((7, CH, 128), F32),
        vmem((1, 1, 768), F32),
        vmem((SPACE, 1, 768), F32),
        vmem((1, 1, CH), F32),
        vmem((SPACE, 1, CH), F32),
        vmem((1, 1, 768), F32),
        vmem((SPACE, 1, 768), F32),
        vmem((1, 1, 768), F32),
        vmem((DP, 1, 768), F32),
        vmem((6, 4, 8, 40, 128), F32),
        vmem((6, 4, 4, 40, 128), F32),
        vmem((6, 3, 4, 48, 128), jnp.int16),
        vmem((6, 3, 4, 48, 128), jnp.int16),
        vmem((6, 4, 40, 128), F32),
        vmem((6, 3, 40, 128), F32),
        vmem((6, 40, 128), F32),
        vmem((6, 4, 40, 128), F32),
        vmem((6, 48, 128), jnp.int16),
        vmem((6, 4, 8, 48, 128), jnp.int16),
        vmem((3, CH, 128), F32),
        pltpu.SemaphoreType.DMA((16,)),
        pltpu.SemaphoreType.DMA((REMOTE,)),
        pltpu.SemaphoreType.DMA((REMOTE,)),
    ]
    shapes = (
        ((ROWS, CH, COLS), BF16),
        ((ROWS, CH, COLS), BF16),
        ((3, 3, CH, CH), F32),
        ((CH, CH), F32),
    )
    held = pl.pallas_call(
        kernel,
        out_shape=tuple(vmem(*shape) for shape in shapes),
        in_specs=[anywhere] * 8,
        out_specs=[pl.BlockSpec(memory_space=pltpu.VMEM)] * 4,
        scratch_shapes=scratch,
        compiler_params=pltpu.CompilerParams(
            collective_id=0, has_side_effects=True, vmem_limit_bytes=52 * 1024 * 1024
        ),
        name="block",
    )(
        embedding.astype(F32).reshape(CH),
        jnp.swapaxes(latent, 2, 3).reshape(ROWS, CH, COLS),
        jnp.swapaxes(cotangent, 2, 3).reshape(ROWS, CH, COLS),
        conv_weight.reshape(3, 3 * CH, CH),
        time_weight,
        norm_gain,
        norm_bias,
        conv_bias,
    )
    out, lg, wgrad, tgrad = pl.pallas_call(
        store,
        out_shape=tuple(jax.ShapeDtypeStruct(*shape) for shape in shapes),
        in_specs=[anywhere] * 4,
        out_specs=[anywhere] * 4,
        scratch_shapes=[pltpu.SemaphoreType.DMA((4,))],
        compiler_params=pltpu.CompilerParams(vmem_limit_bytes=1024 * 1024),
        name="store",
    )(*held)
    out = jnp.swapaxes(out.reshape(1, ROWS, CH, COLS), 2, 3)
    lg = jnp.swapaxes(lg.reshape(1, ROWS, CH, COLS), 2, 3)
    return out, lg, wgrad, tgrad


def solution(mesh):
    wide = P("dp", "space", None, None)
    return jax.shard_map(
        per_device,
        mesh=mesh,
        in_specs=(wide, P("dp"), P(), P(), P(), P(), P(), wide),
        out_specs=(wide, wide, P(), P()),
        check_vma=False,
    )
```

```python
import math

import jax
import jax.numpy as jnp
from jax import lax
from jax.experimental import pallas as pl
from jax.experimental.pallas import tpu as pltpu
from jax.sharding import PartitionSpec as P

GROUPS = 32
EPSILON = 1e-05
CH = 320
ROWS = 4
COLS = 512
CELLS = ROWS * COLS
PER_GROUP = CH // GROUPS
SPACE = 16
DP = 8
DEEP = 1024
MESH = pl.DeviceIdType.MESH
F32 = jnp.float32
BF16 = jnp.bfloat16

HALO = 0
STATS = 4
BACK = STATS + 15
COLUMN = BACK + 15
TIME = COLUMN + 15
REDUCE = TIME + 7
PER_FLOW = 17
REMOTE = REDUCE + 6 * PER_FLOW

HALF_US, TILE_US, EVENT_US = 0.45, 0.75, 0.1
TAP_ROWS = (0, 1, 2)
ARRIVES_US = (2.0, 7.0, 10.0, 13.0, 16.0, 21.0, 23.5)


def from_blocks(blocks):
    wide_blocks = blocks.astype(jnp.int32).astype(F32)
    return wide_blocks[:, :40] * jnp.exp2(wide_blocks[:, 40:41] - 15.0)


def device_at(x, y, z, core):
    return (x * 2 + lax.rem(z, 2), lax.div(z, 2) * 8 + y * 2 + core)


def kernel(
    emb_hbm, x_hbm, g_hbm, w_hbm, tw_hbm, gain_hbm, nbias_hbm, cbias_hbm,
    outb, lgb, res, tgo,
    xb, gb, wb, tw, emb, gain, nbias, cbias,
    wgl, wcl, gt, g3, a3, at, act_s, ng, cols,
    st_out, st_rx, co_out, co_rx, bk_out, bk_rx, tm_out, tm_rx,
    wg, rx0, tx1, rx1, s1, rx2, s2, rx3, fin,
    sums, local, send, recv,
):
    dp = lax.axis_index("dp")
    sp = lax.axis_index("space")
    x = lax.div(dp, 2)
    z = lax.div(sp, 8) * 2 + lax.rem(dp, 2)
    y = lax.rem(lax.div(sp, 2), 4)
    core = lax.rem(sp, 2)
    other = 1 - core
    place = {"x": x, "y": y, "z": z}

    def along(axis, d):
        spot = dict(place)
        spot[axis] = lax.rem(place[axis] + d, 4)
        return spot[axis], device_at(spot["x"], spot["y"], spot["z"], core)

    def space_peer(d):
        return (dp, lax.rem(sp + d, SPACE))

    def dp_peer(d):
        return (lax.rem(dp + d, DP), sp)

    partner = (dp, sp + 1 - 2 * core)

    def remote(number, src, dst, device):
        return pltpu.make_async_remote_copy(
            src_ref=src, dst_ref=dst, send_sem=send.at[number], recv_sem=recv.at[number],
            device_id=device, device_id_type=MESH,
        )

    def load(number, src, dst):
        return pltpu.make_async_copy(src, dst, local.at[number])

    loads = {
        "x": load(0, x_hbm, xb.at[pl.ds(1, ROWS)]),
        "g": load(1, g_hbm, gb.at[pl.ds(1, ROWS)]),
        "tw": load(2, tw_hbm, tw),
        "emb": load(3, emb_hbm, emb),
        "gain": load(4, gain_hbm, gain),
        "nbias": load(5, nbias_hbm, nbias),
        "cbias": load(6, cbias_hbm, cbias),
        "w": load(7, w_hbm, wb),
    }
    barrier = pltpu.get_barrier_semaphore()
    peers = [space_peer(d) for d in range(1, SPACE)] + [dp_peer(d) for d in range(1, DP)]
    peers.append(device_at(x, y, 3 - z, core))
    for peer in peers:
        pl.semaphore_signal(barrier, inc=1, device_id=peer, device_id_type=MESH)

    for name in loads:
        loads[name].start()

    for slot in range(ROWS + 2):
        rows = pl.ds(slot * DEEP + 3 * CH, DEEP - 3 * CH)
        g3[rows, :] = jnp.zeros((DEEP - 3 * CH, COLS), BF16)
        a3[rows, :] = jnp.zeros((DEEP - 3 * CH, COLS), BF16)

    @pl.when(sp == 0)
    def _():
        gb[0] = jnp.zeros((CH, COLS), BF16)

    @pl.when(sp == SPACE - 1)
    def _():
        gb[ROWS + 1] = jnp.zeros((CH, COLS), BF16)

    loads["x"].wait()

    block = 80

    def lane_tiles(ref, rows):
        for r in range(1, ROWS + 1):
            row = ref[r, rows, :].astype(F32)
            for n in range(COLS // 128):
                yield row[:, n * 128 : (n + 1) * 128]

    def local_sums(k, carry):
        rows = pl.ds(pl.multiple_of(k * block, block), block)
        x_sum = sum(lane_tiles(xb, rows), jnp.zeros((block, 128), F32))
        x_mean = jnp.sum(x_sum, axis=1, keepdims=True) * (1.0 / CELLS)
        sums[0, rows, :] = jnp.broadcast_to(x_mean, (block, 128))
        squares = jnp.zeros((block, 128), F32)
        for piece in lane_tiles(xb, rows):
            away = piece - x_mean
            squares = squares + away * away
        sums[1, rows, :] = squares
        return carry

    def local_totals(k, carry):
        rows = pl.ds(pl.multiple_of(k * block, block), block)
        sums[2, rows, :] = sum(lane_tiles(gb, rows), jnp.zeros((block, 128), F32))
        return carry

    lax.fori_loop(0, CH // block, local_sums, 0)
    st_out[0, :, pl.ds(0, CH)] = sums[0].T[0:1]
    st_out[0, :, pl.ds(384, CH)] = jnp.sum(sums[1].T, axis=0, keepdims=True)

    def gather_space(base, out, rx):
        return [
            remote(base + d - 1, out.at[0], rx.at[sp], space_peer(d)) for d in range(1, SPACE)
        ]

    stats = gather_space(STATS, st_out, st_rx)
    pl.semaphore_wait(barrier, len(peers))
    for copy in stats:
        copy.start()
    st_rx[sp] = st_out[0]
    loads["g"].wait()

    up = (dp, lax.max(sp - 1, 0))
    down = (dp, lax.min(sp + 1, SPACE - 1))
    g_up = remote(HALO, gb.at[1], gb.at[ROWS + 1], up)
    g_down = remote(HALO + 1, gb.at[ROWS], gb.at[0], down)
    x_up = remote(HALO + 2, xb.at[1], xb.at[ROWS + 1], up)
    x_down = remote(HALO + 3, xb.at[ROWS], xb.at[0], down)

    @pl.when(sp > 0)
    def _():
        g_up.start()

    @pl.when(sp < SPACE - 1)
    def _():
        g_down.start()

    @pl.when(sp > 0)
    def _():
        x_up.start()

    @pl.when(sp < SPACE - 1)
    def _():
        x_down.start()

    lax.fori_loop(0, CH // block, local_totals, 0)
    co_out[0, :, :] = jnp.sum(sums[2].T, axis=0, keepdims=True)
    columns = gather_space(COLUMN, co_out, co_rx)
    for copy in columns:
        copy.start()
    co_rx[sp] = co_out[0]


    at_col = lax.broadcasted_iota(jnp.int32, (CH, COLS), 1)

    def three(row, towards):
        before = jnp.where(at_col == 0, 0.0, pltpu.roll(row, 1, 1))
        after = jnp.where(at_col == COLS - 1, 0.0, pltpu.roll(row, COLS - 1, 1))
        return (before, row, after) if towards else (after, row, before)

    def spread(ref, k, pieces):
        for j in range(3):
            rows = pl.ds(pl.multiple_of(k * DEEP + j * CH, 64), CH)
            ref[rows, :] = pieces[j].astype(BF16)

    def spread_g(k, carry):
        pieces = three(gb[k].astype(F32), False)
        spread(g3, k, pieces)
        gt[pl.ds(pl.multiple_of(k * COLS, COLS), COLS), :] = (
            g3[pl.ds(pl.multiple_of(k * DEEP, DEEP), DEEP), :].T
        )
        return carry

    lax.fori_loop(1, ROWS + 1, spread_g, 0)
    loads["w"].wait()

    def lay_out(i, carry):
        taps = wb[i].astype(F32)
        none = jnp.zeros((CH, DEEP - 3 * CH), F32)
        wcl[:, pl.ds(pl.multiple_of(i * DEEP, DEEP), DEEP)] = jnp.concatenate(
            [taps.T, none], axis=1
        ).astype(BF16)
        wgl[:, pl.ds(pl.multiple_of((2 - i) * DEEP, DEEP), DEEP)] = jnp.concatenate(
            [taps[0:CH], taps[CH : 2 * CH], taps[2 * CH :], none], axis=1
        ).astype(BF16)
        return carry

    lax.fori_loop(0, 3, lay_out, 0)

    def ends_g():
        @pl.when(sp > 0)
        def _():
            g_up.wait_send()
            g_down.wait_recv()

        @pl.when(sp < SPACE - 1)
        def _():
            g_down.wait_send()
            g_up.wait_recv()

        lax.fori_loop(0, 2, lambda n, carry: spread_g(n * (ROWS + 1), carry), 0)

    ends_g()

    row_of = lax.broadcasted_iota(jnp.int32, (CH, CH), 0)
    col_of = lax.broadcasted_iota(jnp.int32, (CH, CH), 1)
    same = (lax.shift_right_logical(row_of * 6554, 16) == lax.shift_right_logical(col_of * 6554, 16))
    member = same.astype(F32)

    def over_group(rows):
        return jnp.dot(
            jnp.broadcast_to(rows, (8, CH)), member,
            precision=lax.Precision.HIGHEST, preferred_element_type=F32,
        )[0:1]

    def to_column(n, rows):
        cols[n] = jnp.broadcast_to(rows, (128, CH)).T

    for name in ("gain", "nbias", "cbias", "emb", "tw"):
        loads[name].wait()
    to_column(0, gain[...].reshape(1, CH))
    to_column(1, nbias[...].reshape(1, CH))
    time_bias = jnp.dot(
        jnp.broadcast_to(emb[...].reshape(1, CH), (16, CH)).astype(BF16), tw[...],
        preferred_element_type=F32,
    )[0:1]
    to_column(2, cbias[...].reshape(1, CH) + time_bias)
    for copy in stats:
        copy.wait()
    means = [st_rx[s, :, pl.ds(0, CH)] for s in range(SPACE)]
    total = means[0]
    for s in range(1, SPACE):
        total = total + means[s]
    mean = over_group(total) * (1.0 / (SPACE * PER_GROUP))
    around = jnp.zeros((1, CH), F32)
    for s in range(SPACE):
        away = means[s] - mean
        around = around + (st_rx[s, :, pl.ds(384, CH)] + float(CELLS) * (away * away))
    var = over_group(around) * (1.0 / (SPACE * PER_GROUP * CELLS))
    to_column(3, mean)
    to_column(4, lax.rsqrt(var + EPSILON))

    def lanes(n):
        return pl.ds(n * 128, 128)

    def activate(k):
        for n in range(COLS // 128):
            normed = (xb[k, :, lanes(n)].astype(F32) - cols[3]) * cols[4]
            shifted = normed * cols[0] + cols[1]
            act_s[:, lanes(n)] = shifted * jax.nn.sigmoid(shifted)

    def spread_a(k, carry):
        activate(k)
        act = act_s[...]
        at[:, pl.ds(pl.multiple_of((k - 1) * COLS, COLS), COLS)] = act.astype(BF16)
        return carry

    lax.fori_loop(1, ROWS + 1, spread_a, 0)

    for copy in columns:
        copy.wait()
    g_all = co_rx[0]
    for n in range(1, SPACE):
        g_all = g_all + co_rx[n]
    tm_out[0, :, pl.ds(0, CH)] = emb[...].reshape(1, CH)
    tm_out[0, :, pl.ds(384, CH)] = g_all
    times = [
        remote(TIME + d - 1, tm_out.at[0], tm_rx.at[dp], dp_peer(d)) for d in range(1, DP)
    ]
    for copy in times:
        copy.start()
    tm_rx[dp] = tm_out[0]

    def to_blocks(values):
        top = jnp.max(jnp.abs(values), axis=1, keepdims=True)
        power = jnp.ceil(jnp.log2(jnp.maximum(top, 1e-30)) + 0.01)
        whole = jnp.floor(values * jnp.exp2(15.0 - power) + 0.5)
        powers = jnp.broadcast_to(power, (values.shape[0], 8, 128))
        return jnp.concatenate([whole, powers], axis=1).astype(jnp.int32).astype(jnp.int16)

    orders = (("x", "y", "z"), ("y", "z", "x"), ("z", "x", "y"))
    mine = pl.ds(core * 4, 4)
    theirs = pl.ds(other * 4, 4)

    def axes(f):
        names = orders[f % 3]
        return (*names, *[place[name] for name in names])

    def stage(number, f):
        base = REDUCE + f * PER_FLOW
        first_axis, second_axis, third_axis, qa, qb, qc = axes(f)
        if number == 0:
            return [remote(base, wg.at[f, :, theirs], rx0.at[f], partner)]
        if number == 6:
            return [remote(base + 16, res.at[f, :, mine], res.at[f, :, mine], partner)]
        copies = []
        for d in range(1, 4):
            n = base + 1 + (number - 1) * 3 + d - 1
            if number == 1:
                to, device = along(first_axis, d)
                copies.append(remote(n, tx1.at[f, d - 1], rx1.at[f, d - 1], device))
            elif number == 2:
                to, device = along(second_axis, d)
                copies.append(remote(n, s1.at[f, to], rx2.at[f, d - 1], device))
            elif number == 3:
                to, device = along(third_axis, d)
                copies.append(remote(n, s2.at[f], rx3.at[f, qc], device))
            elif number == 4:
                to, device = along(second_axis, d)
                copies.append(remote(n, fin.at[f], res.at[f, qa, core * 4 + qb], device))
            else:
                to, device = along(first_axis, d)
                piece = res.at[f, qa, mine]
                copies.append(remote(n, piece, piece, device))
        return copies

    def start(number, f):
        for copy in stage(number, f):
            copy.start()

    def event(number, f):
        first_axis, second_axis, third_axis, qa, qb, qc = axes(f)
        for copy in stage(number, f):
            copy.wait_recv()
        if number == 0:
            s1[f] = wg[f, qa, mine] + rx0[f, qa]
            for d in range(1, 4):
                to, _ = along(first_axis, d)
                tx1[f, d - 1] = to_blocks(wg[f, to, mine] + rx0[f, to])
        elif number == 1:
            for d in range(3):
                s1[f] += from_blocks(rx1[f, d])
        elif number == 2:
            total = s1[f, qb] + rx2[f, 0] + rx2[f, 1] + rx2[f, 2]
            s2[f] = total
            rx3[f, qc] = total
        elif number == 3:
            total = rx3[f, 0] + rx3[f, 1] + rx3[f, 2] + rx3[f, 3]
            block = to_blocks(total[None])[0]
            fin[f] = block
            res[f, qa, core * 4 + qb] = block
        if number < 6:
            start(number + 1, f)

    flows = 6
    due = sorted(
        (HALF_US * (f + 1) + ARRIVES_US[number], number, f)
        for number in range(7)
        for f in range(flows)
    )
    clock = [0.0]

    def work(us, do):
        while due and due[0][0] <= clock[0]:
            event(*due.pop(0)[1:])
            clock[0] += EVENT_US
        do()
        clock[0] += us

    def weight_part(f):
        c = TAP_ROWS[f // 2]
        for n in range((f % 2) * 2, (f % 2) * 2 + 2):
            part = jnp.dot(
                at[...],
                gt[pl.ds((2 - c) * COLS, CELLS), pl.ds(n * 256, 256)],
                preferred_element_type=F32,
            )
            for side in range(2):
                wg[f, (n % 2) * 2 + side] = part[:, side * 128 : (side + 1) * 128].reshape(
                    8, 40, 128
                )
        start(0, f)

    for f in range(flows):
        work(HALF_US, lambda f=f: weight_part(f))

    def spread_row(k):
        spread(a3, k, three(at[:, pl.ds((k - 1) * COLS, COLS)].astype(F32), True))

    def edge_a(k):
        activate(k)
        spread(a3, k, three(act_s[...], True))

    def blank_a(k):
        a3[pl.ds(k * DEEP, 3 * CH), :] = jnp.zeros((3 * CH, COLS), BF16)

    def top_a():
        @pl.when(sp > 0)
        def _():
            x_up.wait_send()
            x_down.wait_recv()
            edge_a(0)

        @pl.when(sp == 0)
        def _():
            blank_a(0)

    def bottom_a():
        @pl.when(sp < SPACE - 1)
        def _():
            x_down.wait_send()
            x_up.wait_recv()
            edge_a(ROWS + 1)

        @pl.when(sp == SPACE - 1)
        def _():
            blank_a(ROWS + 1)

    wide = 256
    tiles = CELLS // wide

    def spot(t):
        return t // 2, (t % 2) * wide

    def convolve(left, right, t):
        row, col = spot(t)
        rows = pl.ds(row * DEEP, 3 * DEEP)
        return jnp.dot(left[...], right[rows, pl.ds(col, wide)], preferred_element_type=F32)

    def back_tile(t):
        row, col = spot(t)
        grad = convolve(wgl, g3, t)
        for n in range(wide // 128):
            here = pl.ds(col + n * 128, 128)
            normed = (xb[row + 1, :, here].astype(F32) - cols[3]) * cols[4]
            shifted = normed * cols[0] + cols[1]
            sig = jax.nn.sigmoid(shifted)
            n_grad = (
                grad[:, n * 128 : (n + 1) * 128] * sig * (1.0 + shifted * (1.0 - sig)) * cols[0]
            )
            ng[row, :, here] = n_grad
            sums[0] += n_grad
            sums[1] += n_grad * normed

    sums[0] = jnp.zeros((CH, 128), F32)
    sums[1] = jnp.zeros((CH, 128), F32)

    def out_tile(t):
        row, col = spot(t)
        conv = convolve(wcl, a3, t)
        for n in range(wide // 128):
            here = pl.ds(col + n * 128, 128)
            xs = xb[row + 1, :, here].astype(F32)
            outb[row, :, here] = (xs + conv[:, n * 128 : (n + 1) * 128] + cols[2]).astype(BF16)

    def send_back():
        bk_out[0, :, pl.ds(0, CH)] = jnp.sum(sums[0].T, axis=0, keepdims=True)
        bk_out[0, :, pl.ds(384, CH)] = jnp.sum(sums[1].T, axis=0, keepdims=True)
        for copy in gather_space(BACK, bk_out, bk_rx):
            copy.start()
        bk_rx[sp] = bk_out[0]

    def take_back():
        for copy in gather_space(BACK, bk_out, bk_rx):
            copy.wait()
        scale = 1.0 / (SPACE * PER_GROUP * CELLS)
        for n in range(2):
            total = bk_rx[0, :, pl.ds(n * 384, CH)]
            for s in range(1, SPACE):
                total = total + bk_rx[s, :, pl.ds(n * 384, CH)]
            to_column(5 + n, over_group(total) * scale)

    def grad_row(row):
        for n in range(COLS // 128):
            normed = (xb[row + 1, :, lanes(n)].astype(F32) - cols[3]) * cols[4]
            change = cols[4] * (ng[row, :, lanes(n)] - cols[5] - normed * cols[6])
            lgb[row, :, lanes(n)] = (gb[row + 1, :, lanes(n)].astype(F32) + change).astype(BF16)

    def time_gradient():
        for copy in times:
            copy.wait()
        embs = jnp.concatenate([tm_rx[n, :, pl.ds(0, CH)] for n in range(DP)], axis=0)
        grads = jnp.concatenate([tm_rx[n, :, pl.ds(384, CH)] for n in range(DP)], axis=0)
        tgo[...] = lax.dot_general(
            embs, grads, (((0,), (0,)), ((), ())),
            precision=lax.Precision.HIGHEST, preferred_element_type=F32,
        )

    for t in range(tiles):
        work(TILE_US, lambda t=t: back_tile(t))
    work(1.0, send_back)
    work(0.5, top_a)
    work(0.5, bottom_a)
    for k in range(1, ROWS + 1):
        work(0.3, lambda k=k: spread_row(k))
    for t in range(tiles):
        work(TILE_US, lambda t=t: out_tile(t))
    work(1.0, take_back)
    for row in range(ROWS):
        work(0.5, lambda row=row: grad_row(row))
    work(1.0, time_gradient)
    while due:
        event(*due.pop(0)[1:])
    for f in range(flows):
        for number in range(7):
            for copy in stage(number, f):
                copy.wait_send()


def store(out_v, lg_v, res, tg_v, out_hbm, lg_hbm, wg_hbm, tg_hbm, wgo, sems):
    pairs = ((out_v, out_hbm), (lg_v, lg_hbm), (tg_v, tg_hbm))
    copies = [pltpu.make_async_copy(a, b, sems.at[n]) for n, (a, b) in enumerate(pairs)]
    for copy in copies:
        copy.start()
    for n, c in enumerate(TAP_ROWS):
        part = [from_blocks(res[2 * n + m // 4, m % 4]).reshape(CH, 128) for m in range(8)]
        wgo[c, 0] = jnp.concatenate([part[0], part[1], part[2][:, :64]], axis=1)
        wgo[c, 1] = jnp.concatenate([part[2][:, 64:], part[3], part[4]], axis=1)
        wgo[c, 2] = jnp.concatenate([part[5], part[6], part[7][:, :64]], axis=1)
        copies.append(pltpu.make_async_copy(wgo.at[c], wg_hbm.at[c], sems.at[3 + n]))
        copies[-1].start()
    for copy in copies:
        copy.wait()


def per_device(
    latent, timesteps, norm_gain, norm_bias, conv_weight, conv_bias, time_weight, cotangent
):
    half_count = CH // 2
    frequency = jnp.exp(-math.log(10000.0) * jnp.arange(half_count, dtype=F32) / half_count)
    angles = timesteps.astype(F32)[:, None] * frequency[None, :]
    embedding = jnp.concatenate([jnp.cos(angles), jnp.sin(angles)], axis=1).astype(BF16)
    anywhere = pl.BlockSpec(memory_space=pl.ANY)
    vmem = pltpu.VMEM
    scratch = [
        vmem((ROWS + 2, CH, COLS), BF16),
        vmem((ROWS + 2, CH, COLS), BF16),
        vmem((3, 3 * CH, CH), BF16),
        vmem((CH, CH), BF16),
        vmem((CH,), F32),
        vmem((CH,), F32),
        vmem((CH,), F32),
        vmem((CH,), F32),
        vmem((CH, 3 * DEEP), BF16),
        vmem((CH, 3 * DEEP), BF16),
        vmem(((ROWS + 2) * COLS, DEEP), BF16),
        vmem(((ROWS + 2) * DEEP, COLS), BF16),
        vmem(((ROWS + 2) * DEEP, COLS), BF16),
        vmem((CH, CELLS), BF16),
        vmem((CH, COLS), F32),
        vmem((ROWS, CH, COLS), F32),
        vmem((7, CH, 128), F32),
        vmem((1, 1, 768), F32),
        vmem((SPACE, 1, 768), F32),
        vmem((1, 1, CH), F32),
        vmem((SPACE, 1, CH), F32),
        vmem((1, 1, 768), F32),
        vmem((SPACE, 1, 768), F32),
        vmem((1, 1, 768), F32),
        vmem((DP, 1, 768), F32),
        vmem((6, 4, 8, 40, 128), F32),
        vmem((6, 4, 4, 40, 128), F32),
        vmem((6, 3, 4, 48, 128), jnp.int16),
        vmem((6, 3, 4, 48, 128), jnp.int16),
        vmem((6, 4, 40, 128), F32),
        vmem((6, 3, 40, 128), F32),
        vmem((6, 40, 128), F32),
        vmem((6, 4, 40, 128), F32),
        vmem((6, 48, 128), jnp.int16),
        vmem((3, CH, 128), F32),
        pltpu.SemaphoreType.DMA((16,)),
        pltpu.SemaphoreType.DMA((REMOTE,)),
        pltpu.SemaphoreType.DMA((REMOTE,)),
    ]
    shapes = (
        ((ROWS, CH, COLS), BF16),
        ((ROWS, CH, COLS), BF16),
        ((3, 3, CH, CH), F32),
        ((CH, CH), F32),
    )
    held = pl.pallas_call(
        kernel,
        out_shape=tuple(
            vmem(*shape)
            for shape in (*shapes[:2], ((6, 4, 8, 48, 128), jnp.int16), shapes[3])
        ),
        in_specs=[anywhere] * 8,
        out_specs=[pl.BlockSpec(memory_space=pltpu.VMEM)] * 4,
        scratch_shapes=scratch,
        compiler_params=pltpu.CompilerParams(
            collective_id=0, has_side_effects=True, vmem_limit_bytes=52 * 1024 * 1024
        ),
        name="block",
    )(
        embedding.astype(F32).reshape(CH),
        jnp.swapaxes(latent, 2, 3).reshape(ROWS, CH, COLS),
        jnp.swapaxes(cotangent, 2, 3).reshape(ROWS, CH, COLS),
        conv_weight.reshape(3, 3 * CH, CH),
        time_weight,
        norm_gain,
        norm_bias,
        conv_bias,
    )
    out, lg, wgrad, tgrad = pl.pallas_call(
        store,
        out_shape=tuple(jax.ShapeDtypeStruct(*shape) for shape in shapes),
        in_specs=[anywhere, anywhere, pl.BlockSpec(memory_space=pltpu.VMEM), anywhere],
        out_specs=[anywhere] * 4,
        scratch_shapes=[vmem((3, 3, CH, CH), F32), pltpu.SemaphoreType.DMA((6,))],
        compiler_params=pltpu.CompilerParams(vmem_limit_bytes=8 * 1024 * 1024),
        name="store",
    )(*held)
    out = jnp.swapaxes(out.reshape(1, ROWS, CH, COLS), 2, 3)
    lg = jnp.swapaxes(lg.reshape(1, ROWS, CH, COLS), 2, 3)
    return out, lg, wgrad, tgrad


def solution(mesh):
    wide = P("dp", "space", None, None)
    return jax.shard_map(
        per_device,
        mesh=mesh,
        in_specs=(wide, P("dp"), P(), P(), P(), P(), P(), wide),
        out_specs=(wide, wide, P(), P()),
        check_vma=False,
    )
```

```python
import math

import jax
import jax.numpy as jnp
from jax import lax
from jax.experimental import pallas as pl
from jax.experimental.pallas import tpu as pltpu
from jax.sharding import PartitionSpec as P

GROUPS = 32
EPSILON = 1e-05
CH = 320
ROWS = 4
COLS = 512
CELLS = ROWS * COLS
PER_GROUP = CH // GROUPS
SPACE = 16
DP = 8
DEEP = 1024
MESH = pl.DeviceIdType.MESH
F32 = jnp.float32
BF16 = jnp.bfloat16

HALO = 0
STATS = 4
BACK = STATS + 15
COLUMN = BACK + 15
TIME = COLUMN + 15
REDUCE = TIME + 7
PER_FLOW = 17
REMOTE = REDUCE + 6 * PER_FLOW

HALF_US, TILE_US, EVENT_US = 0.45, 0.75, 0.1
TAP_ROWS = (0, 1, 2)
ARRIVES_US = (2.0, 7.0, 10.0, 13.0, 16.0, 21.0, 23.5)


def from_blocks(blocks):
    wide_blocks = blocks.astype(jnp.int32).astype(F32)
    return wide_blocks[:, :40] * jnp.exp2(wide_blocks[:, 40:41] - 15.0)


def device_at(x, y, z, core):
    return (x * 2 + lax.rem(z, 2), lax.div(z, 2) * 8 + y * 2 + core)


def kernel(
    emb_hbm, x_hbm, g_hbm, w_hbm, tw_hbm, gain_hbm, nbias_hbm, cbias_hbm,
    outb, lgb, res, tgo,
    xb, gb, wb, tw, emb, gain, nbias, cbias,
    wgl, wcl, gt, g3, a3, at, act_s, ng, cols,
    st_out, st_rx, co_out, co_rx, bk_out, bk_rx, tm_out, tm_rx,
    wg, rx0, tx1, rx1, s1, rx2, s2, rx3, fin,
    sums, local, send, recv,
):
    dp = lax.axis_index("dp")
    sp = lax.axis_index("space")
    x = lax.div(dp, 2)
    z = lax.div(sp, 8) * 2 + lax.rem(dp, 2)
    y = lax.rem(lax.div(sp, 2), 4)
    core = lax.rem(sp, 2)
    other = 1 - core
    place = {"x": x, "y": y, "z": z}

    def along(axis, d):
        spot = dict(place)
        spot[axis] = lax.rem(place[axis] + d, 4)
        return spot[axis], device_at(spot["x"], spot["y"], spot["z"], core)

    def space_peer(d):
        return (dp, lax.rem(sp + d, SPACE))

    def dp_peer(d):
        return (lax.rem(dp + d, DP), sp)

    partner = (dp, sp + 1 - 2 * core)

    def remote(number, src, dst, device):
        return pltpu.make_async_remote_copy(
            src_ref=src, dst_ref=dst, send_sem=send.at[number], recv_sem=recv.at[number],
            device_id=device, device_id_type=MESH,
        )

    def load(number, src, dst):
        return pltpu.make_async_copy(src, dst, local.at[number])

    loads = {
        "x": load(0, x_hbm, xb.at[pl.ds(1, ROWS)]),
        "g": load(1, g_hbm, gb.at[pl.ds(1, ROWS)]),
        "tw": load(2, tw_hbm, tw),
        "emb": load(3, emb_hbm, emb),
        "gain": load(4, gain_hbm, gain),
        "nbias": load(5, nbias_hbm, nbias),
        "cbias": load(6, cbias_hbm, cbias),
        "w": load(7, w_hbm, wb),
    }
    barrier = pltpu.get_barrier_semaphore()
    peers = [space_peer(d) for d in range(1, SPACE)] + [dp_peer(d) for d in range(1, DP)]
    peers.append(device_at(x, y, 3 - z, core))
    for peer in peers:
        pl.semaphore_signal(barrier, inc=1, device_id=peer, device_id_type=MESH)

    for name in loads:
        loads[name].start()

    for slot in range(ROWS + 2):
        rows = pl.ds(slot * DEEP + 3 * CH, DEEP - 3 * CH)
        g3[rows, :] = jnp.zeros((DEEP - 3 * CH, COLS), BF16)
        a3[rows, :] = jnp.zeros((DEEP - 3 * CH, COLS), BF16)

    @pl.when(sp == 0)
    def _():
        gb[0] = jnp.zeros((CH, COLS), BF16)

    @pl.when(sp == SPACE - 1)
    def _():
        gb[ROWS + 1] = jnp.zeros((CH, COLS), BF16)

    loads["x"].wait()

    block = 80

    def lane_tiles(ref, rows):
        for r in range(1, ROWS + 1):
            row = ref[r, rows, :].astype(F32)
            for n in range(COLS // 128):
                yield row[:, n * 128 : (n + 1) * 128]

    def local_sums(k, carry):
        rows = pl.ds(pl.multiple_of(k * block, block), block)
        x_sum = sum(lane_tiles(xb, rows), jnp.zeros((block, 128), F32))
        x_mean = jnp.sum(x_sum, axis=1, keepdims=True) * (1.0 / CELLS)
        sums[0, rows, :] = jnp.broadcast_to(x_mean, (block, 128))
        squares = jnp.zeros((block, 128), F32)
        for piece in lane_tiles(xb, rows):
            away = piece - x_mean
            squares = squares + away * away
        sums[1, rows, :] = squares
        return carry

    def local_totals(k, carry):
        rows = pl.ds(pl.multiple_of(k * block, block), block)
        sums[2, rows, :] = sum(lane_tiles(gb, rows), jnp.zeros((block, 128), F32))
        return carry

    lax.fori_loop(0, CH // block, local_sums, 0)
    st_out[0, :, pl.ds(0, CH)] = sums[0].T[0:1]
    st_out[0, :, pl.ds(384, CH)] = jnp.sum(sums[1].T, axis=0, keepdims=True)

    def gather_space(base, out, rx):
        return [
            remote(base + d - 1, out.at[0], rx.at[sp], space_peer(d)) for d in range(1, SPACE)
        ]

    stats = gather_space(STATS, st_out, st_rx)
    pl.semaphore_wait(barrier, len(peers))
    for copy in stats:
        copy.start()
    st_rx[sp] = st_out[0]
    loads["g"].wait()

    up = (dp, lax.max(sp - 1, 0))
    down = (dp, lax.min(sp + 1, SPACE - 1))
    g_up = remote(HALO, gb.at[1], gb.at[ROWS + 1], up)
    g_down = remote(HALO + 1, gb.at[ROWS], gb.at[0], down)
    x_up = remote(HALO + 2, xb.at[1], xb.at[ROWS + 1], up)
    x_down = remote(HALO + 3, xb.at[ROWS], xb.at[0], down)

    @pl.when(sp > 0)
    def _():
        g_up.start()

    @pl.when(sp < SPACE - 1)
    def _():
        g_down.start()

    @pl.when(sp > 0)
    def _():
        x_up.start()

    @pl.when(sp < SPACE - 1)
    def _():
        x_down.start()

    lax.fori_loop(0, CH // block, local_totals, 0)
    co_out[0, :, :] = jnp.sum(sums[2].T, axis=0, keepdims=True)
    columns = gather_space(COLUMN, co_out, co_rx)
    for copy in columns:
        copy.start()
    co_rx[sp] = co_out[0]


    at_col = lax.broadcasted_iota(jnp.int32, (CH, COLS), 1)

    def three(row, towards):
        before = jnp.where(at_col == 0, 0.0, pltpu.roll(row, 1, 1))
        after = jnp.where(at_col == COLS - 1, 0.0, pltpu.roll(row, COLS - 1, 1))
        return (before, row, after) if towards else (after, row, before)

    def spread(ref, k, pieces):
        for j in range(3):
            rows = pl.ds(pl.multiple_of(k * DEEP + j * CH, 64), CH)
            ref[rows, :] = pieces[j].astype(BF16)

    def spread_g(k, carry):
        pieces = three(gb[k].astype(F32), False)
        spread(g3, k, pieces)
        gt[pl.ds(pl.multiple_of(k * COLS, COLS), COLS), :] = (
            g3[pl.ds(pl.multiple_of(k * DEEP, DEEP), DEEP), :].T
        )
        return carry

    lax.fori_loop(1, ROWS + 1, spread_g, 0)

    def lay_out(i, carry):
        taps = wb[i].astype(F32)
        none = jnp.zeros((CH, DEEP - 3 * CH), F32)
        wcl[:, pl.ds(i * DEEP, DEEP)] = jnp.concatenate(
            [taps.T, none], axis=1
        ).astype(BF16)
        wgl[:, pl.ds((2 - i) * DEEP, DEEP)] = jnp.concatenate(
            [taps[0:CH], taps[CH : 2 * CH], taps[2 * CH :], none], axis=1
        ).astype(BF16)
        return carry

    def ends_g():
        @pl.when(sp > 0)
        def _():
            g_up.wait_send()
            g_down.wait_recv()

        @pl.when(sp < SPACE - 1)
        def _():
            g_down.wait_send()
            g_up.wait_recv()

        lax.fori_loop(0, 2, lambda n, carry: spread_g(n * (ROWS + 1), carry), 0)

    ends_g()

    row_of = lax.broadcasted_iota(jnp.int32, (CH, CH), 0)
    col_of = lax.broadcasted_iota(jnp.int32, (CH, CH), 1)
    same = (lax.shift_right_logical(row_of * 6554, 16) == lax.shift_right_logical(col_of * 6554, 16))
    member = same.astype(F32)

    def over_group(rows):
        return jnp.dot(
            jnp.broadcast_to(rows, (8, CH)), member,
            precision=lax.Precision.HIGHEST, preferred_element_type=F32,
        )[0:1]

    def to_column(n, rows):
        cols[n] = jnp.broadcast_to(rows, (128, CH)).T

    for name in ("gain", "nbias", "cbias", "emb", "tw"):
        loads[name].wait()
    to_column(0, gain[...].reshape(1, CH))
    to_column(1, nbias[...].reshape(1, CH))
    time_bias = jnp.dot(
        jnp.broadcast_to(emb[...].reshape(1, CH), (16, CH)).astype(BF16), tw[...],
        preferred_element_type=F32,
    )[0:1]
    to_column(2, cbias[...].reshape(1, CH) + time_bias)
    for copy in stats:
        copy.wait()
    means = [st_rx[s, :, pl.ds(0, CH)] for s in range(SPACE)]
    total = means[0]
    for s in range(1, SPACE):
        total = total + means[s]
    mean = over_group(total) * (1.0 / (SPACE * PER_GROUP))
    around = jnp.zeros((1, CH), F32)
    for s in range(SPACE):
        away = means[s] - mean
        around = around + (st_rx[s, :, pl.ds(384, CH)] + float(CELLS) * (away * away))
    var = over_group(around) * (1.0 / (SPACE * PER_GROUP * CELLS))
    to_column(3, mean)
    to_column(4, lax.rsqrt(var + EPSILON))

    def lanes(n):
        return pl.ds(n * 128, 128)

    def activate(k):
        for n in range(COLS // 128):
            normed = (xb[k, :, lanes(n)].astype(F32) - cols[3]) * cols[4]
            shifted = normed * cols[0] + cols[1]
            act_s[:, lanes(n)] = shifted * jax.nn.sigmoid(shifted)

    def spread_a(k, carry):
        activate(k)
        act = act_s[...]
        at[:, pl.ds(pl.multiple_of((k - 1) * COLS, COLS), COLS)] = act.astype(BF16)
        return carry

    lax.fori_loop(1, ROWS + 1, spread_a, 0)

    for copy in columns:
        copy.wait()
    g_all = co_rx[0]
    for n in range(1, SPACE):
        g_all = g_all + co_rx[n]
    tm_out[0, :, pl.ds(0, CH)] = emb[...].reshape(1, CH)
    tm_out[0, :, pl.ds(384, CH)] = g_all
    times = [
        remote(TIME + d - 1, tm_out.at[0], tm_rx.at[dp], dp_peer(d)) for d in range(1, DP)
    ]
    for copy in times:
        copy.start()
    tm_rx[dp] = tm_out[0]

    def to_blocks(values):
        top = jnp.max(jnp.abs(values), axis=1, keepdims=True)
        power = jnp.ceil(jnp.log2(jnp.maximum(top, 1e-30)) + 0.01)
        whole = jnp.floor(values * jnp.exp2(15.0 - power) + 0.5)
        powers = jnp.broadcast_to(power, (values.shape[0], 8, 128))
        return jnp.concatenate([whole, powers], axis=1).astype(jnp.int32).astype(jnp.int16)

    orders = (("x", "y", "z"), ("y", "z", "x"), ("z", "x", "y"))
    mine = pl.ds(core * 4, 4)
    theirs = pl.ds(other * 4, 4)

    def axes(f):
        names = orders[f % 3]
        return (*names, *[place[name] for name in names])

    def stage(number, f):
        base = REDUCE + f * PER_FLOW
        first_axis, second_axis, third_axis, qa, qb, qc = axes(f)
        if number == 0:
            return [remote(base, wg.at[f, :, theirs], rx0.at[f], partner)]
        if number == 6:
            return [remote(base + 16, res.at[f, :, mine], res.at[f, :, mine], partner)]
        copies = []
        for d in range(1, 4):
            n = base + 1 + (number - 1) * 3 + d - 1
            if number == 1:
                to, device = along(first_axis, d)
                copies.append(remote(n, tx1.at[f, d - 1], rx1.at[f, d - 1], device))
            elif number == 2:
                to, device = along(second_axis, d)
                copies.append(remote(n, s1.at[f, to], rx2.at[f, d - 1], device))
            elif number == 3:
                to, device = along(third_axis, d)
                copies.append(remote(n, s2.at[f], rx3.at[f, qc], device))
            elif number == 4:
                to, device = along(second_axis, d)
                copies.append(remote(n, fin.at[f], res.at[f, qa, core * 4 + qb], device))
            else:
                to, device = along(first_axis, d)
                piece = res.at[f, qa, mine]
                copies.append(remote(n, piece, piece, device))
        return copies

    def start(number, f):
        for copy in stage(number, f):
            copy.start()

    def event(number, f):
        first_axis, second_axis, third_axis, qa, qb, qc = axes(f)
        for copy in stage(number, f):
            copy.wait_recv()
        if number == 0:
            s1[f] = wg[f, qa, mine] + rx0[f, qa]
            for d in range(1, 4):
                to, _ = along(first_axis, d)
                tx1[f, d - 1] = to_blocks(wg[f, to, mine] + rx0[f, to])
        elif number == 1:
            for d in range(3):
                s1[f] += from_blocks(rx1[f, d])
        elif number == 2:
            total = s1[f, qb] + rx2[f, 0] + rx2[f, 1] + rx2[f, 2]
            s2[f] = total
            rx3[f, qc] = total
        elif number == 3:
            total = rx3[f, 0] + rx3[f, 1] + rx3[f, 2] + rx3[f, 3]
            block = to_blocks(total[None])[0]
            fin[f] = block
            res[f, qa, core * 4 + qb] = block
        if number < 6:
            start(number + 1, f)

    flows = 6
    due = sorted(
        (HALF_US * (f + 1) + ARRIVES_US[number], number, f)
        for number in range(7)
        for f in range(flows)
    )
    clock = [0.0]

    def work(us, do):
        while due and due[0][0] <= clock[0]:
            event(*due.pop(0)[1:])
            clock[0] += EVENT_US
        do()
        clock[0] += us

    def weight_part(f):
        c = TAP_ROWS[f // 2]
        for n in range((f % 2) * 2, (f % 2) * 2 + 2):
            part = jnp.dot(
                at[...],
                gt[pl.ds((2 - c) * COLS, CELLS), pl.ds(n * 256, 256)],
                preferred_element_type=F32,
            )
            for side in range(2):
                wg[f, (n % 2) * 2 + side] = part[:, side * 128 : (side + 1) * 128].reshape(
                    8, 40, 128
                )
        start(0, f)

    for f in range(flows):
        work(HALF_US, lambda f=f: weight_part(f))

    def spread_row(k):
        spread(a3, k, three(at[:, pl.ds((k - 1) * COLS, COLS)].astype(F32), True))

    def edge_a(k):
        activate(k)
        spread(a3, k, three(act_s[...], True))

    def blank_a(k):
        a3[pl.ds(k * DEEP, 3 * CH), :] = jnp.zeros((3 * CH, COLS), BF16)

    def top_a():
        @pl.when(sp > 0)
        def _():
            x_up.wait_send()
            x_down.wait_recv()
            edge_a(0)

        @pl.when(sp == 0)
        def _():
            blank_a(0)

    def bottom_a():
        @pl.when(sp < SPACE - 1)
        def _():
            x_down.wait_send()
            x_up.wait_recv()
            edge_a(ROWS + 1)

        @pl.when(sp == SPACE - 1)
        def _():
            blank_a(ROWS + 1)

    wide = 256
    tiles = CELLS // wide

    def spot(t):
        return t // 2, (t % 2) * wide

    def convolve(left, right, t):
        row, col = spot(t)
        rows = pl.ds(row * DEEP, 3 * DEEP)
        return jnp.dot(left[...], right[rows, pl.ds(col, wide)], preferred_element_type=F32)

    def back_tile(t):
        row, col = spot(t)
        grad = convolve(wgl, g3, t)
        for n in range(wide // 128):
            here = pl.ds(col + n * 128, 128)
            normed = (xb[row + 1, :, here].astype(F32) - cols[3]) * cols[4]
            shifted = normed * cols[0] + cols[1]
            sig = jax.nn.sigmoid(shifted)
            n_grad = (
                grad[:, n * 128 : (n + 1) * 128] * sig * (1.0 + shifted * (1.0 - sig)) * cols[0]
            )
            ng[row, :, here] = n_grad
            sums[0] += n_grad
            sums[1] += n_grad * normed

    sums[0] = jnp.zeros((CH, 128), F32)
    sums[1] = jnp.zeros((CH, 128), F32)

    def out_tile(t):
        row, col = spot(t)
        conv = convolve(wcl, a3, t)
        for n in range(wide // 128):
            here = pl.ds(col + n * 128, 128)
            xs = xb[row + 1, :, here].astype(F32)
            outb[row, :, here] = (xs + conv[:, n * 128 : (n + 1) * 128] + cols[2]).astype(BF16)

    def send_back():
        bk_out[0, :, pl.ds(0, CH)] = jnp.sum(sums[0].T, axis=0, keepdims=True)
        bk_out[0, :, pl.ds(384, CH)] = jnp.sum(sums[1].T, axis=0, keepdims=True)
        for copy in gather_space(BACK, bk_out, bk_rx):
            copy.start()
        bk_rx[sp] = bk_out[0]

    def take_back():
        for copy in gather_space(BACK, bk_out, bk_rx):
            copy.wait()
        scale = 1.0 / (SPACE * PER_GROUP * CELLS)
        for n in range(2):
            total = bk_rx[0, :, pl.ds(n * 384, CH)]
            for s in range(1, SPACE):
                total = total + bk_rx[s, :, pl.ds(n * 384, CH)]
            to_column(5 + n, over_group(total) * scale)

    def grad_row(row):
        for n in range(COLS // 128):
            normed = (xb[row + 1, :, lanes(n)].astype(F32) - cols[3]) * cols[4]
            change = cols[4] * (ng[row, :, lanes(n)] - cols[5] - normed * cols[6])
            lgb[row, :, lanes(n)] = (gb[row + 1, :, lanes(n)].astype(F32) + change).astype(BF16)

    def time_gradient():
        for copy in times:
            copy.wait()
        embs = jnp.concatenate([tm_rx[n, :, pl.ds(0, CH)] for n in range(DP)], axis=0)
        grads = jnp.concatenate([tm_rx[n, :, pl.ds(384, CH)] for n in range(DP)], axis=0)
        tgo[...] = lax.dot_general(
            embs, grads, (((0,), (0,)), ((), ())),
            precision=lax.Precision.HIGHEST, preferred_element_type=F32,
        )

    loads["w"].wait()
    for i in range(3):
        work(0.4, lambda i=i: lay_out(i, 0))
    for t in range(tiles):
        work(TILE_US, lambda t=t: back_tile(t))
    work(1.0, send_back)
    work(0.5, top_a)
    work(0.5, bottom_a)
    for k in range(1, ROWS + 1):
        work(0.3, lambda k=k: spread_row(k))
    for t in range(tiles):
        work(TILE_US, lambda t=t: out_tile(t))
    work(1.0, take_back)
    for row in range(ROWS):
        work(0.5, lambda row=row: grad_row(row))
    work(1.0, time_gradient)
    while due:
        event(*due.pop(0)[1:])
    for f in range(flows):
        for number in range(7):
            for copy in stage(number, f):
                copy.wait_send()


def store(out_v, lg_v, res, tg_v, out_hbm, lg_hbm, wg_hbm, tg_hbm, wgo, sems):
    pairs = ((out_v, out_hbm), (lg_v, lg_hbm), (tg_v, tg_hbm))
    copies = [pltpu.make_async_copy(a, b, sems.at[n]) for n, (a, b) in enumerate(pairs)]
    for copy in copies:
        copy.start()
    for n, c in enumerate(TAP_ROWS):
        part = [from_blocks(res[2 * n + m // 4, m % 4]).reshape(CH, 128) for m in range(8)]
        wgo[c, 0] = jnp.concatenate([part[0], part[1], part[2][:, :64]], axis=1)
        wgo[c, 1] = jnp.concatenate([part[2][:, 64:], part[3], part[4]], axis=1)
        wgo[c, 2] = jnp.concatenate([part[5], part[6], part[7][:, :64]], axis=1)
        copies.append(pltpu.make_async_copy(wgo.at[c], wg_hbm.at[c], sems.at[3 + n]))
        copies[-1].start()
    for copy in copies:
        copy.wait()


def per_device(
    latent, timesteps, norm_gain, norm_bias, conv_weight, conv_bias, time_weight, cotangent
):
    half_count = CH // 2
    frequency = jnp.exp(-math.log(10000.0) * jnp.arange(half_count, dtype=F32) / half_count)
    angles = timesteps.astype(F32)[:, None] * frequency[None, :]
    embedding = jnp.concatenate([jnp.cos(angles), jnp.sin(angles)], axis=1).astype(BF16)
    anywhere = pl.BlockSpec(memory_space=pl.ANY)
    vmem = pltpu.VMEM
    scratch = [
        vmem((ROWS + 2, CH, COLS), BF16),
        vmem((ROWS + 2, CH, COLS), BF16),
        vmem((3, 3 * CH, CH), BF16),
        vmem((CH, CH), BF16),
        vmem((CH,), F32),
        vmem((CH,), F32),
        vmem((CH,), F32),
        vmem((CH,), F32),
        vmem((CH, 3 * DEEP), BF16),
        vmem((CH, 3 * DEEP), BF16),
        vmem(((ROWS + 2) * COLS, DEEP), BF16),
        vmem(((ROWS + 2) * DEEP, COLS), BF16),
        vmem(((ROWS + 2) * DEEP, COLS), BF16),
        vmem((CH, CELLS), BF16),
        vmem((CH, COLS), F32),
        vmem((ROWS, CH, COLS), F32),
        vmem((7, CH, 128), F32),
        vmem((1, 1, 768), F32),
        vmem((SPACE, 1, 768), F32),
        vmem((1, 1, CH), F32),
        vmem((SPACE, 1, CH), F32),
        vmem((1, 1, 768), F32),
        vmem((SPACE, 1, 768), F32),
        vmem((1, 1, 768), F32),
        vmem((DP, 1, 768), F32),
        vmem((6, 4, 8, 40, 128), F32),
        vmem((6, 4, 4, 40, 128), F32),
        vmem((6, 3, 4, 48, 128), jnp.int16),
        vmem((6, 3, 4, 48, 128), jnp.int16),
        vmem((6, 4, 40, 128), F32),
        vmem((6, 3, 40, 128), F32),
        vmem((6, 40, 128), F32),
        vmem((6, 4, 40, 128), F32),
        vmem((6, 48, 128), jnp.int16),
        vmem((3, CH, 128), F32),
        pltpu.SemaphoreType.DMA((16,)),
        pltpu.SemaphoreType.DMA((REMOTE,)),
        pltpu.SemaphoreType.DMA((REMOTE,)),
    ]
    shapes = (
        ((ROWS, CH, COLS), BF16),
        ((ROWS, CH, COLS), BF16),
        ((3, 3, CH, CH), F32),
        ((CH, CH), F32),
    )
    held = pl.pallas_call(
        kernel,
        out_shape=tuple(
            vmem(*shape)
            for shape in (*shapes[:2], ((6, 4, 8, 48, 128), jnp.int16), shapes[3])
        ),
        in_specs=[anywhere] * 8,
        out_specs=[pl.BlockSpec(memory_space=pltpu.VMEM)] * 4,
        scratch_shapes=scratch,
        compiler_params=pltpu.CompilerParams(
            collective_id=0, has_side_effects=True, vmem_limit_bytes=52 * 1024 * 1024
        ),
        name="block",
    )(
        embedding.astype(F32).reshape(CH),
        jnp.swapaxes(latent, 2, 3).reshape(ROWS, CH, COLS),
        jnp.swapaxes(cotangent, 2, 3).reshape(ROWS, CH, COLS),
        conv_weight.reshape(3, 3 * CH, CH),
        time_weight,
        norm_gain,
        norm_bias,
        conv_bias,
    )
    out, lg, wgrad, tgrad = pl.pallas_call(
        store,
        out_shape=tuple(jax.ShapeDtypeStruct(*shape) for shape in shapes),
        in_specs=[anywhere, anywhere, pl.BlockSpec(memory_space=pltpu.VMEM), anywhere],
        out_specs=[anywhere] * 4,
        scratch_shapes=[vmem((3, 3, CH, CH), F32), pltpu.SemaphoreType.DMA((6,))],
        compiler_params=pltpu.CompilerParams(vmem_limit_bytes=8 * 1024 * 1024),
        name="store",
    )(*held)
    out = jnp.swapaxes(out.reshape(1, ROWS, CH, COLS), 2, 3)
    lg = jnp.swapaxes(lg.reshape(1, ROWS, CH, COLS), 2, 3)
    return out, lg, wgrad, tgrad


def solution(mesh):
    wide = P("dp", "space", None, None)
    return jax.shard_map(
        per_device,
        mesh=mesh,
        in_specs=(wide, P("dp"), P(), P(), P(), P(), P(), wide),
        out_specs=(wide, wide, P(), P()),
        check_vma=False,
    )
```
